32 devices in a mesh: grp: 8 (over z, core), sub: 4 (over y, x).
Axes of the slice: x: 2, y: 2, z: 4, core: 2. Of those that a mesh axis runs over, the one named last changes fastest.
Arguments:
- right_side: float32 [8, 4, 512, 128], P('grp', 'sub'), may hold values from -6 to 6
- live_rows: int32 [8, 4], P('grp', 'sub'), may hold values from 384 to 512, as said below
- margin_blocks: int32 [8, 4, 2], P('grp', 'sub'), may hold values from 0 to 5, as said below
- local_operator: bfloat16 [8, 4, 640, 640], P('grp', 'sub'), may hold values from -0.25 to 0.25
- local_inverse: bfloat16 [8, 4, 640, 640], P('grp', 'sub'), may hold values from -0.25 to 0.25
- deflation: bfloat16 [8, 4, 640, 16], P('grp', 'sub'), may hold values from -0.5 to 0.5
- coarse_inverse: bfloat16 [512, 512], P('grp', 'sub'), may hold values from -0.25 to 0.25
Outputs:
- solution_field: float32 [8, 4, 512, 128], P('grp', 'sub')
- residual: float32 [8, 4, 512, 128], P('grp', 'sub')
The draws below stay inside these ranges and needn't reach their ends.
Inputs may be any that keep to these rules, and one draw needn't show every extreme that they name: `live_rows`: some subdomain has 512 live rows and some has 384. `margin_blocks`: the two blocks a subdomain lends differ.
All inputs are finite; a program needn't handle non-finite values.
Results may differ from the reference program's by a relative error of at most 0.015.
Values may be sent and summed in bfloat16 or wider, within the bound.
No kernel may reach another device: no remote copies, remote signals or barrier semaphores. Data moves between devices by JAX's collectives and lax.ppermute only.
A program may use at most 64 MiB of HBM per device.

```python
import jax
import jax.numpy as jnp
from jax import lax

NLOC = 640
BLK = 64
DEFL = 16
LOADS = 128
ITERS = 3
OWN = 512
NC = 512
N_GRP = 8
N_SUB = 4


def draw_live_rows(key, part):
    lowest = NLOC - 4 * BLK
    highest = NLOC - 2 * BLK
    total = N_GRP * N_SUB
    key_one, key_two, key_three = jax.random.split(key, 3)
    values = jax.random.randint(key_one, (total,), lowest, highest + 1, dtype=jnp.int32)
    top_spot = jax.random.randint(key_two, (), 0, total, dtype=jnp.int32)
    low_spot = (top_spot + jax.random.randint(key_three, (), 1, total, dtype=jnp.int32)) % total
    places = jnp.arange(total, dtype=jnp.int32)
    values = jnp.where(places == top_spot, highest, values)
    values = jnp.where(places == low_spot, lowest, values)
    return values.reshape(N_GRP, N_SUB).astype(jnp.int32)


def draw_margin_blocks(key, part):
    block_count = (NLOC - 4 * BLK) // BLK
    key_one, key_two = jax.random.split(jax.random.fold_in(key, 7))
    first_block = jax.random.randint(key_one, (N_GRP, N_SUB), 0, block_count, dtype=jnp.int32)
    offset = jax.random.randint(key_two, (N_GRP, N_SUB), 1, block_count, dtype=jnp.int32)
    second_block = (first_block + offset) % block_count
    return jnp.stack([first_block, second_block], axis=-1).astype(jnp.int32)


def steps_of(key, shape, shards, smallest, largest):
    def one(dim, parts):
        heights = jax.random.uniform(jax.random.fold_in(jax.random.fold_in(key, 6), dim), (parts,), jnp.float32, smallest / len(shards), largest / len(shards))
        return jnp.repeat(jnp.exp(heights), shape[dim] // parts).reshape((-1,) + (1,) * (len(shape) - dim - 1))

    gain = one(*shards[0])
    for cut in shards[1:]:
        gain = gain * one(*cut)
    return gain


def bell_draw(rng, extent, scale, bound, shards=(), held_as=jnp.bfloat16):
    drawn = jax.random.normal(rng, extent, jnp.float32) * scale
    if len(shards) > 0:
        drawn = steps_of(rng, extent, shards, -0.22, 0.18) * drawn
    return jnp.clip(drawn, min=-bound, max=bound).astype(held_as)


def setup_inputs(seed: int = 0) -> dict:
    streams_of = jax.random.split(jax.random.key(seed), 8)
    return {
        "right_side": bell_draw(streams_of[0], (N_GRP, N_SUB, OWN, LOADS), 1.0, 6.0, ((0, 8), (1, 4)), jnp.float32),
        "live_rows": draw_live_rows(jax.random.fold_in(streams_of[7], 71), 0),
        "margin_blocks": draw_margin_blocks(jax.random.fold_in(streams_of[7], 71), 0),
        "local_operator": bell_draw(streams_of[3], (N_GRP, N_SUB, NLOC, NLOC), NLOC ** -0.5, 0.25, ((0, 8), (1, 4))),
        "local_inverse": bell_draw(streams_of[4], (N_GRP, N_SUB, NLOC, NLOC), NLOC ** -0.5, 0.25, ((0, 8), (1, 4))),
        "deflation": bell_draw(streams_of[5], (N_GRP, N_SUB, NLOC, DEFL), 0.08, 0.5, ((0, 8), (1, 4))),
        "coarse_inverse": bell_draw(streams_of[6], (NC, NC), NC ** -0.5, 0.25, ((0, 8), (1, 4))),
    }


STEP_SIZES = (0.8, 0.9, 1.0)
MOMENTUM = (0.0, 0.3, 0.3)


def both_axes(function):
    return jax.vmap(jax.vmap(function))


def take_block(vector, block_index):
    return lax.dynamic_slice_in_dim(vector, block_index.astype(jnp.int32) * BLK, BLK, 0)


def add_block(vector, block_index, addend):
    first_row = block_index.astype(jnp.int32) * BLK
    current = lax.dynamic_slice_in_dim(vector, first_row, BLK, 0)
    return lax.dynamic_update_slice_in_dim(vector, current + addend, first_row, 0)


def spread_rows(vector, give_right, give_left):
    to_right = both_axes(take_block)(vector, give_right)
    to_left = both_axes(take_block)(vector, give_left)
    empty = jnp.zeros_like(to_right[:, :1])
    from_left = jnp.concatenate([empty, to_right[:, :-1]], axis=1)
    from_right = jnp.concatenate([to_left[:, 1:], empty], axis=1)
    return jnp.concatenate([vector, from_left, from_right], axis=2)


def collect_rows(local, give_right, give_left, live_mask):
    owned = local[:, :, :OWN] * live_mask
    to_left = local[:, :, OWN:OWN + BLK]
    to_right = local[:, :, OWN + BLK:]
    empty = jnp.zeros_like(to_left[:, :1])
    from_left = jnp.concatenate([empty, to_right[:, :-1]], axis=1)
    from_right = jnp.concatenate([to_left[:, 1:], empty], axis=1)
    owned = both_axes(add_block)(owned, give_left, from_left)
    return both_axes(add_block)(owned, give_right, from_right)


def apply_local(matrices, vectors, form):
    def one_group(pair):
        return jnp.einsum(form, pair[0].astype(jnp.float32), pair[1].astype(jnp.float32),
                          precision=lax.Precision.HIGHEST)
    return lax.map(one_group, (matrices, vectors))


def coarse_apply(coarse_inverse, ordered):
    bands = coarse_inverse.reshape(N_GRP, N_SUB * DEFL, NC)
    column = ordered.astype(jnp.float32)

    def one_band(band):
        return jnp.dot(band.astype(jnp.float32), column, precision=lax.Precision.HIGHEST)
    return lax.map(one_band, bands).reshape(N_GRP, N_SUB, DEFL, LOADS)


def reference(right_side, live_rows, margin_blocks, local_operator, local_inverse, deflation, coarse_inverse):
    row_ids = jnp.arange(OWN, dtype=jnp.int32)[None, None, :, None]
    live_mask = (row_ids < live_rows[:, :, None, None]).astype(jnp.float32)
    give_right = margin_blocks[:, :, 0]
    give_left = margin_blocks[:, :, 1]
    residual = right_side * live_mask
    solution = jnp.zeros_like(residual)
    direction = jnp.zeros_like(residual)
    for turn_index in range(ITERS):
        local_resid = spread_rows(residual, give_right, give_left).astype(jnp.bfloat16)
        fine_part = apply_local(local_inverse, local_resid, "sij,sjl->sil")
        coarse_resid = apply_local(deflation, local_resid, "sji,sjl->sil").astype(jnp.bfloat16)
        ordered = jnp.transpose(coarse_resid, (1, 0, 2, 3)).reshape(NC, LOADS)
        coarse_corr = coarse_apply(coarse_inverse, ordered).astype(jnp.bfloat16)
        local_error = fine_part + apply_local(deflation, coarse_corr, "sij,sjl->sil")
        update = collect_rows(local_error, give_right, give_left, live_mask)
        direction = update + MOMENTUM[turn_index] * direction
        solution = solution + STEP_SIZES[turn_index] * direction
        local_dir = spread_rows(direction, give_right, give_left).astype(jnp.bfloat16)
        applied = collect_rows(apply_local(local_operator, local_dir, "sij,sjl->sil"),
                               give_right, give_left, live_mask)
        residual = residual - STEP_SIZES[turn_index] * applied
    return solution, residual
```

```python
import jax
import jax.numpy as jnp
from jax import lax
from jax.sharding import PartitionSpec as P

ITERS = 3


STEP_SIZES = (0.8, 0.9, 1.0)
MOMENTUM = (0.0, 0.3, 0.3)


def body(
    right_side, live_rows, margin_blocks, local_operator, local_inverse, deflation, coarse_inverse
):
    bf16 = jnp.bfloat16
    f32 = jnp.float32
    source = right_side[0, 0]
    owned, loads = source.shape
    operator = local_operator[0, 0]
    inverse = local_inverse[0, 0]
    vectors = deflation[0, 0]
    order, modes = vectors.shape
    blk = (order - owned) // 2
    blocks = owned // blk
    groups = lax.axis_size("grp")
    subs = lax.axis_size("sub")
    position = lax.axis_index("sub")
    has_left = position > 0
    has_right = position < subs - 1
    mask = jnp.arange(owned, dtype=jnp.int32)[:, None] < live_rows[0, 0]
    give_right = margin_blocks[0, 0, 0]
    give_left = margin_blocks[0, 0, 1]
    forward = [(i, (i + 1) % subs) for i in range(subs)]
    backward = [(target, origin) for origin, target in forward]

    def lent(rows, index):
        return lax.dynamic_slice_in_dim(rows, index * blk, blk, 0)

    ids = jnp.arange(blocks, dtype=jnp.int32)[:, None, None]

    def add_lent(owned_part, from_left, from_right):
        tall = owned_part.reshape(blocks, blk, loads)
        tall = tall + jnp.where(ids == give_left, from_left[None], 0.0)
        tall = tall + jnp.where(ids == give_right, from_right[None], 0.0)
        return tall.reshape(owned, loads)

    def swap(rows):
        to_right = jnp.concatenate([rows[owned + blk :], lent(rows, give_right)], axis=0)
        to_left = jnp.concatenate([rows[owned : owned + blk], lent(rows, give_left)], axis=0)
        return (
            lax.ppermute(to_right.astype(bf16), "sub", forward),
            lax.ppermute(to_left.astype(bf16), "sub", backward),
        )

    def joined(rows, from_left, from_right):
        own = add_lent(jnp.where(mask, rows[:owned], 0.0), from_left[:blk], from_right[:blk])
        left = jnp.where(has_left, rows[owned : owned + blk] + from_left[blk:], 0.0)
        right = jnp.where(has_right, rows[owned + blk :] + from_right[blk:], 0.0)
        return jnp.concatenate([own, left, right], axis=0)

    residual = jnp.where(mask, source, 0.0)
    near = min(subs, 3)
    starts = [min(max(k - 1, 0), subs - near) for k in range(subs)]
    columns = coarse_inverse.shape[1]
    wide = near * modes * columns // loads
    panels = [
        coarse_inverse[first * modes : (first + near) * modes].reshape(wide, loads)
        for first in starts
    ]
    to_right = jnp.concatenate(
        [
            vectors[owned + blk :].T,
            lent(vectors, give_right).T,
        ],
        axis=1,
    )
    to_left = jnp.concatenate(
        [
            vectors[owned : owned + blk].T,
            lent(vectors, give_left).T,
        ],
        axis=1,
    )
    ahead = jnp.concatenate([to_right, lent(residual, give_right).astype(bf16)], axis=0)
    behind = jnp.concatenate([to_left, lent(residual, give_left).astype(bf16)], axis=0)
    slots = jnp.arange(subs, dtype=jnp.int32)[:, None, None]
    slots = jnp.where(slots > position, ahead[None], behind[None])
    slots = jnp.concatenate([jnp.stack(panels), slots], axis=1)
    slots = lax.all_to_all(slots, "sub", 0, 0, tiled=True)
    coarse = slots[:, :wide].reshape(subs, near * modes, columns)
    base = jnp.clip(position - 1, 0, subs - near)
    left_slot = jnp.where(
        has_left, lax.dynamic_index_in_dim(slots, jnp.maximum(position - 1, 0), 0, False), 0
    )
    right_slot = jnp.where(
        has_right, lax.dynamic_index_in_dim(slots, jnp.minimum(position + 1, subs - 1), 0, False), 0
    )
    left_vectors = left_slot[wide : wide + modes].T
    right_vectors = right_slot[wide : wide + modes].T
    residual = jnp.concatenate(
        [residual, left_slot[wide + modes :].astype(f32), right_slot[wide + modes :].astype(f32)],
        axis=0,
    )
    solution = jnp.zeros_like(source)
    direction = 0.0
    for turn in range(ITERS):
        local_resid = residual.astype(bf16)
        fine = jnp.dot(inverse, local_resid, preferred_element_type=f32)
        coarse_resid = lax.dot_general(
            vectors, local_resid, (((0,), (0,)), ((), ())), preferred_element_type=f32
        ).astype(bf16)
        from_left, from_right = swap(fine)
        every = jnp.broadcast_to(coarse_resid[None], (subs * groups, modes, loads))
        every = lax.all_to_all(every, ("sub", "grp"), 0, 0, tiled=True).reshape(
            subs, groups * modes, loads
        )
        corrections = sum(
            jnp.dot(coarse[k], every[k], preferred_element_type=f32) for k in range(subs)
        ).astype(bf16)

        def correction(offset):
            row = jnp.clip(position + offset - base, 0, near - 1) * modes
            return lax.dynamic_slice_in_dim(corrections, row, modes, 0)

        update = joined(
            fine + jnp.dot(vectors, correction(0), preferred_element_type=f32),
            jnp.where(has_left, from_left.astype(f32), 0.0)
            + jnp.dot(left_vectors, correction(-1), preferred_element_type=f32),
            jnp.where(has_right, from_right.astype(f32), 0.0)
            + jnp.dot(right_vectors, correction(1), preferred_element_type=f32),
        )
        direction = update + MOMENTUM[turn] * direction
        solution = solution + STEP_SIZES[turn] * direction[:owned]
        applied = jnp.dot(operator, direction.astype(bf16), preferred_element_type=f32)
        from_left, from_right = swap(applied)
        applied = joined(
            applied,
            jnp.where(has_left, from_left.astype(f32), 0.0),
            jnp.where(has_right, from_right.astype(f32), 0.0),
        )
        residual = residual - STEP_SIZES[turn] * applied
    return (solution[None, None], residual[None, None, :owned])


def solution(mesh):
    return jax.shard_map(
        body,
        mesh=mesh,
        in_specs=(
            P("grp", "sub", None, None),
            P("grp", "sub"),
            P("grp", "sub", None),
            P("grp", "sub", None, None),
            P("grp", "sub", None, None),
            P("grp", "sub", None, None),
            P("grp", "sub"),
        ),
        out_specs=(P("grp", "sub", None, None), P("grp", "sub", None, None)),
        check_vma=False,
    )
```

```python
import functools

import jax
import jax.numpy as jnp
from jax import lax
from jax.experimental import pallas as pl
from jax.experimental.pallas import tpu as pltpu
from jax.sharding import PartitionSpec as P

ITERS = 3


STEP_SIZES = (0.8, 0.9, 1.0)
MOMENTUM = (0.0, 0.3, 0.3)

F32 = jnp.float32
BF16 = jnp.bfloat16


def mm(a, b):
    return jnp.dot(a, b, preferred_element_type=F32)


def tn(a, b):
    return lax.dot_general(a, b, (((0,), (0,)), ((), ())), preferred_element_type=F32)


def nt(a, b):
    return lax.dot_general(a, b, (((1,), (1,)), ((), ())), preferred_element_type=F32)


def run(kernel, name, outs, args, scalars=(), scratch=(), flops=1 << 22):
    nbytes = sum(x.size * x.dtype.itemsize for x in args) + sum(
        x.size * jnp.dtype(x.dtype).itemsize for x in outs
    )
    return pl.pallas_call(
        kernel,
        name=name,
        out_shape=outs,
        in_specs=[pl.BlockSpec(memory_space=pltpu.SMEM)] * len(scalars)
        + [pl.BlockSpec(memory_space=pltpu.VMEM)] * len(args),
        out_specs=[pl.BlockSpec(memory_space=pltpu.VMEM)] * len(outs),
        scratch_shapes=list(scratch),
        compiler_params=pltpu.CompilerParams(vmem_limit_bytes=24 << 20),
        cost_estimate=pl.CostEstimate(flops=flops, bytes_accessed=nbytes, transcendentals=0),
    )(*scalars, *args)


def shape(*dims, dtype=F32):
    return jax.ShapeDtypeStruct(dims, dtype)


class Sizes:
    def __init__(self, right_side, deflation, coarse_inverse):
        self.owned, self.loads = right_side.shape[-2:]
        self.order, self.modes = deflation.shape[-2:]
        self.blk = (self.order - self.owned) // 2
        self.subs = lax.axis_size("sub")
        self.groups = lax.axis_size("grp")
        self.near = min(self.subs, 5)
        self.chunks = coarse_inverse.shape[1] // self.loads
        self.window = self.near * self.modes
        self.wide = self.window * self.chunks

    def base(self, position):
        return jnp.clip(position - 2, 0, self.subs - self.near)


class Place:
    def __init__(self, z, margin, live):
        self.z = z
        self.position = lax.axis_index("sub")
        self.give_right = pl.multiple_of(margin[0, 0, 0] * z.blk, z.blk)
        self.give_left = pl.multiple_of(margin[0, 0, 1] * z.blk, z.blk)
        self.live = live[0, 0]
        self.has_left = self.position > 0
        self.has_right = self.position < z.subs - 1
        self.has_left2 = self.position > 1
        self.has_right2 = self.position < z.subs - 2

    def row_mask(self):
        z = self.z
        rows = lax.broadcasted_iota(jnp.int32, (z.owned, z.loads), 0)
        return rows < self.live

    def right_block(self, ref):
        return ref[pl.ds(self.give_right, self.z.blk), :]

    def left_block(self, ref):
        return ref[pl.ds(self.give_left, self.z.blk), :]

    def ahead(self, ref):
        z = self.z
        return jnp.concatenate([ref[z.owned + z.blk :, :], self.right_block(ref)], axis=0)

    def behind(self, ref):
        z = self.z
        return jnp.concatenate([ref[z.owned : z.owned + z.blk, :], self.left_block(ref)], axis=0)


def first_kernel(z, margin, live, source, vectors, panel, slots, own):
    at = Place(z, margin, live)
    own[...] = jnp.where(at.row_mask(), source[...], 0.0)
    side = 2 * z.blk
    eye = (
        lax.broadcasted_iota(jnp.int32, (side, side), 0)
        == lax.broadcasted_iota(jnp.int32, (side, side), 1)
    ).astype(BF16)
    ahead = jnp.concatenate(
        [tn(at.ahead(vectors), eye).astype(BF16), at.right_block(own).astype(BF16)], axis=0
    )
    behind = jnp.concatenate(
        [tn(at.behind(vectors), eye).astype(BF16), at.left_block(own).astype(BF16)], axis=0
    )
    for k in range(z.subs):
        first = min(max(k - 2, 0), z.subs - z.near) * z.modes
        for chunk in range(z.chunks):
            slots[k, chunk * z.window : (chunk + 1) * z.window, :] = panel[
                chunk, first : first + z.window, :
            ]
        slots[k, z.wide :, :] = jnp.where(k > at.position, ahead, behind)


def put_coarse(z, every_out, value):
    value = value.astype(BF16)

    def put(k, carry):
        every_out[k] = value
        return carry

    lax.fori_loop(0, z.subs * z.groups, put, 0, unroll=8)


def second_kernel(z, slots, own, vectors_t, resid, resid_low, every_out):
    position = lax.axis_index("sub")
    left = slots[jnp.maximum(position - 1, 0), z.wide + z.modes :, :]
    right = slots[jnp.minimum(position + 1, z.subs - 1), z.wide + z.modes :, :]
    value = jnp.concatenate(
        [
            own[...],
            jnp.where(position > 0, left.astype(F32), 0.0),
            jnp.where(position < z.subs - 1, right.astype(F32), 0.0),
        ],
        axis=0,
    )
    resid[...] = value
    low = value.astype(BF16)
    resid_low[...] = low
    put_coarse(z, every_out, mm(vectors_t[...], low))


def static_kernel(z, margin, live, operator, vectors_t, picked, ahead, behind):
    at = Place(z, margin, live)
    side = 2 * z.blk
    rows = jnp.concatenate([at.ahead(operator), at.behind(operator)], axis=0)
    picked[...] = rows
    row = lax.broadcasted_iota(jnp.int32, (z.order, side), 0)
    col = lax.broadcasted_iota(jnp.int32, (z.order, side), 1)
    on_left = jnp.where(col < z.blk, at.give_left + col, z.owned - z.blk + col)
    on_right = jnp.where(col < z.blk, at.give_right + col, z.owned + col)
    left_cols = mm(rows, (row == on_left).astype(BF16)).astype(BF16)
    right_cols = mm(rows, (row == on_right).astype(BF16)).astype(BF16)
    col = lax.broadcasted_iota(jnp.int32, (z.modes, z.order), 1)
    limit = jnp.where(at.has_left, z.owned + z.blk, z.owned)
    kept = (col < at.live) | ((col >= z.owned) & (col < limit))
    kept = kept | ((col >= z.owned + z.blk) & at.has_right)
    lifted = nt(jnp.where(kept, vectors_t[...].astype(F32), 0.0).astype(BF16), rows).astype(BF16)
    ahead[...] = jnp.concatenate([left_cols[:side], right_cols[:side], lifted[:, :side]], axis=0)
    behind[...] = jnp.concatenate([right_cols[side:], left_cols[side:], lifted[:, side:]], axis=0)


def window_kernel(z, turn, *refs):
    margin, live, resid_low, inverse, picked, *rest = refs
    old = rest.pop(0) if turn else None
    statics = None if turn else (rest.pop(0), rest.pop(0))
    fine, ahead, behind, *far = rest
    at = Place(z, margin, live)
    side = 2 * z.blk
    fine[...] = mm(inverse[...], resid_low[...])
    part = jnp.concatenate(
        [
            jnp.where(at.row_mask(), fine[: z.owned, :], 0.0),
            jnp.where(at.has_left, fine[z.owned : z.owned + z.blk, :], 0.0),
            jnp.where(at.has_right, fine[z.owned + z.blk :, :], 0.0),
        ],
        axis=0,
    )
    if turn:
        part = part + MOMENTUM[turn] * old[...]
    product = mm(picked[...], part.astype(BF16)).astype(BF16)
    to_right = at.ahead(fine).astype(BF16)
    to_left = at.behind(fine).astype(BF16)
    ahead[:side, :] = to_right
    ahead[side : 2 * side, :] = product[:side]
    behind[:side, :] = to_left
    behind[side : 2 * side, :] = product[side:]
    if statics:
        ahead[2 * side :, :] = statics[0][...]
        behind[2 * side :, :] = statics[1][...]
    if far:
        far[0][...] = jnp.where(at.has_right2, to_right, to_left)


def main_kernel(z, turn, *refs):
    last = turn == ITERS - 1
    margin, live, every, slots, vectors, operator, fine, *rest = refs
    left, right, far_left, far_right, left_static, right_static, resid_in, *rest = rest
    if turn:
        old, solution_in, *rest = rest
    if not last:
        vectors_t, *rest = rest
        direction, solution, resid, resid_low, every_out, error, coarse = rest
    else:
        solution, resid_out, direction, resid, error, coarse = rest
    at = Place(z, margin, live)
    owned, blk, side, modes = z.owned, z.blk, 2 * z.blk, z.modes
    cols = slice(None)

    total = jnp.zeros((z.window, z.loads), F32)
    for k in range(z.subs):
        for chunk in range(z.chunks):
            total = total + mm(
                slots[k, chunk * z.window : (chunk + 1) * z.window, :],
                every[k, chunk * z.loads : (chunk + 1) * z.loads, :],
            )
    coarse[...] = total.astype(BF16)

    def correction(offset):
        index = jnp.clip(at.position + offset - z.base(at.position), 0, z.near - 1)
        return coarse[pl.ds(pl.multiple_of(index * modes, modes), modes), :]

    def their_vectors(offset):
        index = jnp.clip(at.position + offset, 0, z.subs - 1)
        return slots[index, z.wide : z.wide + modes, :]

    def halo(have, piece, offset):
        value = piece.astype(F32) + tn(their_vectors(offset), correction(offset))
        return jnp.where(have, value, 0.0)

    error[...] = fine[...] + mm(vectors[...], correction(0))
    from_left = halo(at.has_left, left[:side, cols], -1)
    from_right = halo(at.has_right, right[:side, cols], 1)
    from_left2 = halo(at.has_left2, far_left[:side, cols], -2)
    from_right2 = halo(at.has_right2, far_right[:side, cols], 2)
    to_right = at.ahead(error).astype(BF16)
    to_left = at.behind(error).astype(BF16)

    mask = at.row_mask()

    def join(target, scale, before, rows, from_left, from_right):
        lower = slice(owned, owned + blk)
        upper = slice(owned + blk, owned + side)
        own = jnp.where(mask, rows[:owned, :], 0.0)
        low = jnp.where(at.has_left, rows[lower, :] + from_left[blk:], 0.0)
        high = jnp.where(at.has_right, rows[upper, :] + from_right[blk:], 0.0)
        parts = ((slice(0, owned), own), (lower, low), (upper, high))
        for span, part in parts:
            part = part if scale == 1.0 else scale * part
            target[span, :] = part if before is None else before(span) + part
        first, second = from_left[:blk], from_right[:blk]
        if scale != 1.0:
            first, second = scale * first, scale * second
        spot = pl.ds(at.give_left, blk)
        target[spot, :] = target[spot, :] + first
        spot = pl.ds(at.give_right, blk)
        target[spot, :] = target[spot, :] + second

    before = (lambda span: MOMENTUM[turn] * old[span, :]) if turn else None
    join(direction, 1.0, before, error, from_left, from_right)
    step = STEP_SIZES[turn] * direction[:owned, :]
    solution[...] = solution_in[...] + step if turn else step

    error[...] = mm(operator[...], direction[...].astype(BF16))

    def borrowed(have, piece, statics, far, near, offset):
        value = (
            piece[side : 2 * side, cols].astype(F32)
            + mm(statics[2 * side : 3 * side, cols], far.astype(BF16))
            + mm(statics[3 * side : 4 * side, cols], near)
            + tn(statics[4 * side :, cols], correction(offset))
        )
        return jnp.where(have, value, 0.0)

    from_left = borrowed(at.has_left, left, left_static, from_left2, to_left, -1)
    from_right = borrowed(at.has_right, right, right_static, from_right2, to_right, 1)
    join(resid, -STEP_SIZES[turn], lambda span: resid_in[span, :], error, from_left, from_right)
    if last:
        resid_out[...] = resid[:owned, :]
    else:
        low = resid[...].astype(BF16)
        resid_low[...] = low
        put_coarse(z, every_out, mm(vectors_t[...], low))


def body(
    right_side, live_rows, margin_blocks, local_operator, local_inverse, deflation, coarse_inverse
):
    z = Sizes(right_side, deflation, coarse_inverse)
    source = right_side[0, 0]
    operator = local_operator[0, 0]
    inverse = local_inverse[0, 0]
    vectors = deflation[0, 0]
    scalars = (margin_blocks, live_rows)
    owned, order, loads, modes = z.owned, z.order, z.loads, z.modes
    side = 2 * z.blk
    rim = 4 * side + modes
    devices = z.subs * z.groups

    def ring(offset):
        return [(i, (i + offset) % z.subs) for i in range(z.subs)]

    def part(function, *more):
        return functools.partial(function, z, *more)

    panel = coarse_inverse.reshape(-1, z.chunks, loads).swapaxes(0, 1)
    slots, own = run(
        part(first_kernel),
        "first",
        [shape(z.subs, z.wide + modes + z.blk, loads, dtype=BF16), shape(owned, loads)],
        [source, vectors, panel],
        scalars,
    )
    slots = lax.all_to_all(slots, "sub", 0, 0, tiled=True)
    vectors_t = vectors.T
    picked, ahead_static, behind_static = run(
        part(static_kernel),
        "static",
        [shape(2 * side, order, dtype=BF16)] + [shape(2 * side + modes, loads, dtype=BF16)] * 2,
        [operator, vectors_t],
        scalars,
    )
    every_shape = shape(devices, modes, loads, dtype=BF16)
    resid, resid_low, every = run(
        part(second_kernel),
        "second",
        [shape(order, loads), shape(order, loads, dtype=BF16), every_shape],
        [slots, own, vectors_t],
    )
    direction = solution = statics = None
    for turn in range(ITERS):
        last = turn == ITERS - 1
        every = lax.all_to_all(every, ("sub", "grp"), 0, 0, tiled=True)
        every = every.reshape(z.subs, z.groups * modes, loads)
        width = 2 * side if turn else rim
        sent = [shape(order, loads)] + [shape(width, loads, dtype=BF16)] * 2
        folded = z.subs == 4
        fine, ahead, behind, *far = run(
            part(window_kernel, turn),
            f"window{turn}",
            sent + [shape(side, loads, dtype=BF16)] * folded,
            [resid_low, inverse, picked]
            + ([direction] if turn else [ahead_static, behind_static]),
            scalars,
        )
        left = lax.ppermute(ahead, "sub", ring(1))
        right = lax.ppermute(behind, "sub", ring(-1))
        if folded:
            far_left = far_right = lax.ppermute(far[0], "sub", ring(2))
        else:
            far_left = lax.ppermute(ahead[:side], "sub", ring(2))
            far_right = lax.ppermute(behind[:side], "sub", ring(-2))
        if not turn:
            statics = (left, right)
        work = [pltpu.VMEM((order, loads), F32), pltpu.VMEM((z.window, loads), BF16)]
        args = [every, slots, vectors, operator, fine, left, right, far_left, far_right]
        args += [*statics, resid]
        if turn:
            args += [direction, solution]
        if last:
            solution, resid = run(
                part(main_kernel, turn),
                f"main{turn}",
                [shape(owned, loads)] * 2,
                args,
                scalars,
                [pltpu.VMEM((order, loads), F32)] * 2 + work,
            )
        else:
            direction, solution, resid, resid_low, every = run(
                part(main_kernel, turn),
                f"main{turn}",
                [
                    shape(order, loads),
                    shape(owned, loads),
                    shape(order, loads),
                    shape(order, loads, dtype=BF16),
                    every_shape,
                ],
                args + [vectors_t],
                scalars,
                work,
            )
    return (solution[None, None], resid[None, None])


def solution(mesh):
    return jax.shard_map(
        body,
        mesh=mesh,
        in_specs=(
            P("grp", "sub", None, None),
            P("grp", "sub"),
            P("grp", "sub", None),
            P("grp", "sub", None, None),
            P("grp", "sub", None, None),
            P("grp", "sub", None, None),
            P("grp", "sub"),
        ),
        out_specs=(P("grp", "sub", None, None), P("grp", "sub", None, None)),
        check_vma=False,
    )
```

```python
import functools

import jax
import jax.numpy as jnp
from jax import lax
from jax.experimental import pallas as pl
from jax.experimental.pallas import tpu as pltpu
from jax.sharding import PartitionSpec as P

ITERS = 3


STEP_SIZES = (0.8, 0.9, 1.0)
MOMENTUM = (0.0, 0.3, 0.3)

F32 = jnp.float32
BF16 = jnp.bfloat16


def mm(a, b):
    return jnp.dot(a, b, preferred_element_type=F32)


def tn(a, b):
    return lax.dot_general(a, b, (((0,), (0,)), ((), ())), preferred_element_type=F32)


def nt(a, b):
    return lax.dot_general(a, b, (((1,), (1,)), ((), ())), preferred_element_type=F32)


def run(kernel, name, outs, args, scalars=(), scratch=(), flops=1 << 22):
    nbytes = sum(x.size * x.dtype.itemsize for x in map(bare, [*args, *outs]))
    return pl.pallas_call(
        kernel,
        name=name,
        out_shape=[held(x) for x in outs],
        in_specs=[pl.BlockSpec(memory_space=pltpu.SMEM)] * len(scalars) + [spec(x) for x in args],
        out_specs=[spec(x) for x in outs],
        scratch_shapes=list(scratch),
        compiler_params=pltpu.CompilerParams(vmem_limit_bytes=24 << 20),
        cost_estimate=pl.CostEstimate(flops=flops, bytes_accessed=nbytes, transcendentals=0),
    )(
        *scalars,
        *map(given, args),
    )


class Far:
    def __init__(self, array):
        self.array = array


def bare(x):
    return x.array if isinstance(x, Far) else x


def held(x):
    return pltpu.HBM(x.array.shape, x.array.dtype) if isinstance(x, Far) else x


def given(x):
    return pltpu.with_memory_space_constraint(x.array, pltpu.HBM) if isinstance(x, Far) else x


def spec(x):
    return pl.BlockSpec(memory_space=pltpu.HBM if isinstance(x, Far) else pltpu.VMEM)


def shape(*dims, dtype=F32):
    return jax.ShapeDtypeStruct(dims, dtype)


class Sizes:
    def __init__(self, right_side, deflation, coarse_inverse):
        self.owned, self.loads = right_side.shape[-2:]
        self.order, self.modes = deflation.shape[-2:]
        self.blk = (self.order - self.owned) // 2
        self.subs = lax.axis_size("sub")
        self.groups = lax.axis_size("grp")
        self.near = min(self.subs, 5)
        self.chunks = coarse_inverse.shape[1] // self.loads
        self.window = self.near * self.modes
        self.wide = self.window * self.chunks

    def base(self, position):
        return jnp.clip(position - 2, 0, self.subs - self.near)


class Place:
    def __init__(self, z, margin, live):
        self.z = z
        self.position = lax.axis_index("sub")
        self.give_right = pl.multiple_of(margin[0, 0] * z.blk, z.blk) if margin is not None else None
        self.give_left = pl.multiple_of(margin[0, 1] * z.blk, z.blk) if margin is not None else None
        self.live = live[0, 0]
        self.has_left = self.position > 0
        self.has_right = self.position < z.subs - 1
        self.has_left2 = self.position > 1
        self.has_right2 = self.position < z.subs - 2

    def row_mask(self):
        z = self.z
        rows = lax.broadcasted_iota(jnp.int32, (z.owned, z.loads), 0)
        return rows < self.live

    def kept(self, value):
        z = self.z
        low = value[z.owned : z.owned + z.blk]
        high = value[z.owned + z.blk :]
        return jnp.concatenate(
            [
                jnp.where(self.row_mask(), value[: z.owned], 0.0),
                jnp.where(self.has_left, low, 0.0),
                jnp.where(self.has_right, high, 0.0),
            ],
            axis=0,
        )

    def right_block(self, ref):
        return ref[pl.ds(self.give_right, self.z.blk), :]

    def left_block(self, ref):
        return ref[pl.ds(self.give_left, self.z.blk), :]

    def ahead(self, ref):
        z = self.z
        return jnp.concatenate([ref[z.owned + z.blk :, :], self.right_block(ref)], axis=0)

    def behind(self, ref):
        z = self.z
        return jnp.concatenate([ref[z.owned : z.owned + z.blk, :], self.left_block(ref)], axis=0)


def selection(z, block, rim):
    row = lax.broadcasted_iota(jnp.int32, (z.order, 2 * z.blk), 0)
    col = lax.broadcasted_iota(jnp.int32, (z.order, 2 * z.blk), 1)
    return (row == jnp.where(col < z.blk, block + col, rim - z.blk + col)).astype(BF16)


def swapped(z, block, rim):
    row = lax.broadcasted_iota(jnp.int32, (z.order, 2 * z.blk), 0)
    col = lax.broadcasted_iota(jnp.int32, (z.order, 2 * z.blk), 1)
    return (row == jnp.where(col < z.blk, rim + col, block - z.blk + col)).astype(BF16)


def first_kernel(z, live, source_far, vectors_far, panel_far, margin_far, slots, own, *scratch):
    source, vectors_t, panel, margin, sem = scratch
    loads = [
        pltpu.make_async_copy(far, near, sem.at[k])
        for k, (far, near) in enumerate(
            (
                (margin_far, margin),
                (vectors_far, vectors_t),
                (panel_far, panel),
                (source_far, source),
            )
        )
    ]
    for load in loads:
        load.start()
    loads[0].wait()
    at = Place(z, margin, live)
    right_rows = swapped(z, at.give_right, z.owned + z.blk)
    left_rows = swapped(z, at.give_left, z.owned)
    loads[1].wait()
    ahead_vectors = mm(vectors_t[...], right_rows).astype(BF16)
    behind_vectors = mm(vectors_t[...], left_rows).astype(BF16)
    loads[2].wait()
    loads[3].wait()
    own[...] = jnp.where(at.row_mask(), source[...], 0.0)
    ahead = jnp.concatenate([ahead_vectors, at.right_block(own).astype(BF16)], axis=0)
    behind = jnp.concatenate([behind_vectors, at.left_block(own).astype(BF16)], axis=0)
    for k in range(z.subs):
        first = min(max(k - 2, 0), z.subs - z.near) * z.modes
        for chunk in range(z.chunks):
            slots[k, chunk * z.window : (chunk + 1) * z.window, :] = panel[
                chunk, first : first + z.window, :
            ]
        slots[k, z.wide :, :] = jnp.where(k > at.position, ahead, behind)


def static_kernel(z, live, operator, vectors_t, margin_in, ahead, behind, margin, sem):
    load = pltpu.make_async_copy(margin_in, margin, sem)
    load.start()
    load.wait()
    at = Place(z, margin, live)
    side = 2 * z.blk
    rows = jnp.concatenate([at.ahead(operator), at.behind(operator)], axis=0)
    left_cols = mm(rows, selection(z, at.give_left, z.owned)).astype(BF16)
    right_cols = mm(rows, selection(z, at.give_right, z.owned + z.blk)).astype(BF16)
    col = lax.broadcasted_iota(jnp.int32, (z.modes, z.order), 1)
    limit = jnp.where(at.has_left, z.owned + z.blk, z.owned)
    kept = (col < at.live) | ((col >= z.owned) & (col < limit))
    kept = kept | ((col >= z.owned + z.blk) & at.has_right)
    lifted = nt(jnp.where(kept, vectors_t[...].astype(F32), 0.0).astype(BF16), rows).astype(BF16)
    ahead[...] = jnp.concatenate([left_cols[:side], right_cols[:side], lifted[:, :side]], axis=0)
    behind[...] = jnp.concatenate([right_cols[side:], left_cols[side:], lifted[:, side:]], axis=0)


def send_coarse(z, vectors_t, low, copies, every_out, sem):
    value = mm(vectors_t[...], low).astype(BF16)

    def put(k, carry):
        copies[k] = value
        return carry

    lax.fori_loop(0, z.subs * z.groups, put, 0, unroll=8)
    copy = pltpu.make_async_copy(copies, every_out, sem)
    copy.start()
    return copy


def lookahead(at, momentum, low, inverse, operator, part, ahead, behind, far):
    z = at.z
    side = 2 * z.blk
    part_value = mm(inverse[...], low)
    part[...] = part_value
    to_right = at.ahead(part).astype(BF16)
    to_left = at.behind(part).astype(BF16)
    value = at.kept(part_value)
    if momentum is not None:
        value = value + momentum
    part[...] = value
    rows = jnp.concatenate([at.ahead(operator), at.behind(operator)], axis=0)
    product = mm(rows, value.astype(BF16)).astype(BF16)
    ahead[:side, :] = to_right
    ahead[side : 2 * side, :] = product[:side]
    behind[:side, :] = to_left
    behind[side : 2 * side, :] = product[side:]
    if far:
        far[0][...] = jnp.where(at.has_right2, to_right, to_left)


def second_kernel(z, live, slots, own, vectors_t, inverse_far, operator, margin_in, *rest):
    ahead_static, behind_static, resid, every_out, part, ahead, behind, *rest = rest
    far, (inverse, copies, margin, sem) = rest[:-4], rest[-4:]
    load = pltpu.make_async_copy(inverse_far, inverse, sem.at[0])
    load.start()
    load_margin = pltpu.make_async_copy(margin_in, margin, sem.at[2])
    load_margin.start()
    at = Place(z, None, live)
    left = slots[jnp.maximum(at.position - 1, 0), z.wide + z.modes :, :]
    right = slots[jnp.minimum(at.position + 1, z.subs - 1), z.wide + z.modes :, :]
    value = jnp.concatenate(
        [
            own[...],
            jnp.where(at.has_left, left.astype(F32), 0.0),
            jnp.where(at.has_right, right.astype(F32), 0.0),
        ],
        axis=0,
    )
    resid[...] = value
    low = value.astype(BF16)
    store = send_coarse(z, vectors_t, low, copies, every_out, sem.at[1])
    load_margin.wait()
    at = Place(z, margin, live)
    load.wait()
    lookahead(at, None, low, inverse, operator, part, ahead, behind, far)
    ahead[4 * z.blk :, :] = ahead_static[...]
    behind[4 * z.blk :, :] = behind_static[...]
    store.wait()


def main_kernel(z, turn, *refs):
    last = turn == ITERS - 1
    live, every, slots, vectors_t, operator, margin_in, part_in, *rest = refs
    ahead_in, behind_in, left, right, far_left, far_right, *rest = rest
    left_static, right_static, resid_in, *rest = rest
    if turn:
        solution_far, *rest = rest
    if last:
        solution_out, resid_out, direction, resid, solution, error, coarse, margin, sem = rest
    else:
        inverse_far, *rest = rest
        solution_out, resid, every_out, part, ahead, behind, *rest = rest
        far = rest[:-8]
        direction, solution, error, coarse, inverse, copies, margin, sem = rest[-8:]
        load = pltpu.make_async_copy(inverse_far, inverse, sem.at[2])
        load.start()
    if turn:
        load_solution = pltpu.make_async_copy(solution_far, solution, sem.at[0])
        load_solution.start()
    load_margin = pltpu.make_async_copy(margin_in, margin, sem.at[4])
    load_margin.start()
    at = Place(z, None, live)
    owned, blk, side, modes = z.owned, z.blk, 2 * z.blk, z.modes
    cols = slice(None)

    total = jnp.zeros((z.window, z.loads), F32)
    for k in range(z.subs):
        for chunk in range(z.chunks):
            total = total + mm(
                slots[k, chunk * z.window : (chunk + 1) * z.window, :],
                every[k, chunk * z.loads : (chunk + 1) * z.loads, :],
            )
    coarse[...] = total.astype(BF16)

    def correction(offset):
        index = jnp.clip(at.position + offset - z.base(at.position), 0, z.near - 1)
        return coarse[pl.ds(pl.multiple_of(index * modes, modes), modes), :]

    def their_vectors(offset):
        index = jnp.clip(at.position + offset, 0, z.subs - 1)
        return slots[index, z.wide : z.wide + modes, :]

    def halo(have, piece, offset):
        value = piece.astype(F32) + tn(their_vectors(offset), correction(offset))
        return jnp.where(have, value, 0.0)

    lifted = tn(vectors_t[...], correction(0))
    error[...] = lifted
    from_left = halo(at.has_left, left[:side, cols], -1)
    from_right = halo(at.has_right, right[:side, cols], 1)
    from_left2 = halo(at.has_left2, far_left[:side, cols], -2)
    from_right2 = halo(at.has_right2, far_right[:side, cols], 2)
    load_margin.wait()
    at = Place(z, margin, live)
    to_right = (ahead_in[:side, cols].astype(F32) + at.ahead(error)).astype(BF16)
    to_left = (behind_in[:side, cols].astype(F32) + at.behind(error)).astype(BF16)

    def join(target, before, scale, rows, from_left, from_right):
        def scaled(value):
            return value if scale == 1.0 else scale * value

        low = jnp.where(at.has_left, scaled(from_left[blk:]), 0.0)
        high = jnp.where(at.has_right, scaled(from_right[blk:]), 0.0)
        target[...] = before + scaled(at.kept(rows))
        for spot, value in (
            (slice(owned, owned + blk), low),
            (slice(owned + blk, owned + side), high),
            (pl.ds(at.give_left, blk), scaled(from_left[:blk])),
            (pl.ds(at.give_right, blk), scaled(from_right[:blk])),
        ):
            target[spot, :] = target[spot, :] + value

    join(direction, part_in[...], 1.0, lifted, from_left, from_right)
    step = STEP_SIZES[turn] * direction[:owned, :]
    if turn:
        load_solution.wait()
        step = solution[...] + step
    solution[...] = step
    store_solution = pltpu.make_async_copy(solution, solution_out, sem.at[1])
    store_solution.start()

    def borrowed(have, piece, statics, far, near, offset):
        value = (
            piece[side : 2 * side, cols].astype(F32)
            + mm(statics[2 * side : 3 * side, cols], far.astype(BF16))
            + mm(statics[3 * side : 4 * side, cols], near)
            + tn(statics[4 * side :, cols], correction(offset))
        )
        return jnp.where(have, value, 0.0)

    from_left = borrowed(at.has_left, left, left_static, from_left2, to_left, -1)
    from_right = borrowed(at.has_right, right, right_static, from_right2, to_right, 1)
    applied = mm(operator[...], direction[...].astype(BF16))
    join(resid, resid_in[...], -STEP_SIZES[turn], applied, from_left, from_right)
    if last:
        store = pltpu.make_async_copy(resid.at[pl.ds(0, owned), :], resid_out, sem.at[0])
        store.start()
        store.wait()
    else:
        low = resid[...].astype(BF16)
        store = send_coarse(z, vectors_t, low, copies, every_out, sem.at[3])
        load.wait()
        momentum = MOMENTUM[turn + 1] * direction[...]
        lookahead(at, momentum, low, inverse, operator, part, ahead, behind, far)
        store.wait()
    store_solution.wait()


def body(
    right_side, live_rows, margin_blocks, local_operator, local_inverse, deflation, coarse_inverse
):
    z = Sizes(right_side, deflation, coarse_inverse)
    source = right_side[0, 0]
    operator = local_operator[0, 0]
    inverse = Far(local_inverse[0, 0])
    scalars = (live_rows,)
    margin = margin_blocks.reshape(1, -1)
    vectors_t = deflation[0, 0].T
    pick = pltpu.SMEM(margin.shape, jnp.int32)
    sems = pltpu.SemaphoreType.DMA
    owned, order, loads, modes = z.owned, z.order, z.loads, z.modes
    side = 2 * z.blk
    devices = z.subs * z.groups
    folded = z.subs == 4

    def ring(offset):
        return [(i, (i + offset) % z.subs) for i in range(z.subs)]

    def part(function, *more):
        return functools.partial(function, z, *more)

    panel = coarse_inverse.reshape(-1, z.chunks, loads).swapaxes(0, 1)
    slots, own = run(
        part(first_kernel),
        "first",
        [shape(z.subs, z.wide + modes + z.blk, loads, dtype=BF16), shape(owned, loads)],
        [Far(source), Far(vectors_t), Far(panel), Far(margin)],
        scalars,
        [
            pltpu.VMEM(source.shape, F32),
            pltpu.VMEM(vectors_t.shape, BF16),
            pltpu.VMEM(panel.shape, BF16),
            pick,
            sems((4,)),
        ],
    )
    slots = lax.all_to_all(slots, "sub", 0, 0, tiled=True)
    ahead_static, behind_static = run(
        part(static_kernel),
        "static",
        [shape(2 * side + modes, loads, dtype=BF16)] * 2,
        [operator, vectors_t, margin],
        scalars,
        [pick, sems(())],
    )
    full = shape(order, loads)
    next_outs = [full, Far(shape(devices, modes, loads, dtype=BF16)), full]
    next_outs += [shape(2 * side, loads, dtype=BF16)] * 2 + [shape(side, loads, dtype=BF16)] * folded
    next_work = [
        pltpu.VMEM((order, order), BF16),
        pltpu.VMEM((devices, modes, loads), BF16),
        pick,
        sems((5,)),
    ]
    resid, every, error, ahead, behind, *far = run(
        part(second_kernel),
        "second",
        next_outs[:3] + [shape(4 * side + modes, loads, dtype=BF16)] * 2 + next_outs[5:],
        [slots, own, vectors_t, inverse, operator, margin, ahead_static, behind_static],
        scalars,
        next_work,
    )
    solution = statics = None
    for turn in range(ITERS):
        last = turn == ITERS - 1
        every = lax.all_to_all(every, ("sub", "grp"), 0, 0, tiled=True)
        every = every.reshape(z.subs, z.groups * modes, loads)
        left = lax.ppermute(ahead, "sub", ring(1))
        right = lax.ppermute(behind, "sub", ring(-1))
        if folded:
            far_left = far_right = lax.ppermute(far[0], "sub", ring(2))
        else:
            far_left = lax.ppermute(ahead[:side], "sub", ring(2))
            far_right = lax.ppermute(behind[:side], "sub", ring(-2))
        if not turn:
            statics = (left, right)
        args = [every, slots, vectors_t, operator, margin, error, ahead, behind]
        args += [left, right, far_left, far_right, *statics, resid]
        if turn:
            args += [Far(solution)]
        work = [
            pltpu.VMEM((owned, loads), F32),
            pltpu.VMEM((order, loads), F32),
            pltpu.VMEM((z.window, loads), BF16),
        ]
        if last:
            solution, resid = run(
                part(main_kernel, turn),
                f"main{turn}",
                [Far(shape(owned, loads))] * 2,
                args,
                scalars,
                [pltpu.VMEM((order, loads), F32)] * 2 + work + [pick, sems((5,))],
            )
        else:
            solution, resid, every, error, ahead, behind, *far = run(
                part(main_kernel, turn),
                f"main{turn}",
                [Far(shape(owned, loads))] + next_outs,
                args + [inverse],
                scalars,
                [pltpu.VMEM((order, loads), F32)] + work + next_work,
            )
    return (solution[None, None], resid[None, None])


def solution(mesh):
    return jax.shard_map(
        body,
        mesh=mesh,
        in_specs=(
            P("grp", "sub", None, None),
            P("grp", "sub"),
            P("grp", "sub", None),
            P("grp", "sub", None, None),
            P("grp", "sub", None, None),
            P("grp", "sub", None, None),
            P("grp", "sub"),
        ),
        out_specs=(P("grp", "sub", None, None), P("grp", "sub", None, None)),
        check_vma=False,
    )
```

```python
import functools

import jax
import jax.numpy as jnp
from jax import lax
from jax.experimental import pallas as pl
from jax.experimental.pallas import tpu as pltpu
from jax.sharding import PartitionSpec as P

ITERS = 3


STEP_SIZES = (0.8, 0.9, 1.0)
MOMENTUM = (0.0, 0.3, 0.3)

F32 = jnp.float32
BF16 = jnp.bfloat16


def mm(a, b):
    return jnp.dot(a, b, preferred_element_type=F32)


def tn(a, b):
    return lax.dot_general(a, b, (((0,), (0,)), ((), ())), preferred_element_type=F32)


def nt(a, b):
    return lax.dot_general(a, b, (((1,), (1,)), ((), ())), preferred_element_type=F32)


def run(kernel, name, outs, args, scalars=(), scratch=(), flops=1 << 22, aliases=None):
    nbytes = sum(x.size * x.dtype.itemsize for x in map(bare, [*args, *outs]))
    return pl.pallas_call(
        kernel,
        name=name,
        out_shape=[held(x) for x in outs],
        in_specs=[pl.BlockSpec(memory_space=pltpu.SMEM)] * len(scalars) + [spec(x) for x in args],
        out_specs=[spec(x) for x in outs],
        scratch_shapes=list(scratch),
        input_output_aliases=aliases or {},
        compiler_params=pltpu.CompilerParams(vmem_limit_bytes=24 << 20),
        cost_estimate=pl.CostEstimate(flops=flops, bytes_accessed=nbytes, transcendentals=0),
    )(
        *scalars,
        *map(given, args),
    )


class Far:
    def __init__(self, array):
        self.array = array


def bare(x):
    return x.array if isinstance(x, Far) else x


def held(x):
    return pltpu.HBM(x.array.shape, x.array.dtype) if isinstance(x, Far) else x


def given(x):
    return pltpu.with_memory_space_constraint(x.array, pltpu.HBM) if isinstance(x, Far) else x


def spec(x):
    return pl.BlockSpec(memory_space=pltpu.HBM if isinstance(x, Far) else pltpu.VMEM)


def shape(*dims, dtype=F32):
    return jax.ShapeDtypeStruct(dims, dtype)


class Sizes:
    def __init__(self, right_side, deflation, coarse_inverse):
        self.owned, self.loads = right_side.shape[-2:]
        self.order, self.modes = deflation.shape[-2:]
        self.blk = (self.order - self.owned) // 2
        self.side = 2 * self.blk
        self.subs = lax.axis_size("sub")
        self.groups = lax.axis_size("grp")
        self.near = min(self.subs, 5)
        self.chunks = coarse_inverse.shape[1] // self.loads
        self.window = self.near * self.modes
        self.wide = self.window * self.chunks
        self.picked = 2 * self.side
        self.stack = self.modes + 2 * self.picked
        self.folded = self.subs == 4
        self.segments = max(6, 2 + self.order // self.side)

    def base(self, position):
        return jnp.clip(position - 2, 0, self.subs - self.near)


class Place:
    def __init__(self, z, live, margin=None):
        self.z = z
        self.position = lax.axis_index("sub")
        self.even = self.position % 2 == 0
        self.live = live[0, 0]
        self.has_left = self.position > 0
        self.has_right = self.position < z.subs - 1
        self.has_left2 = self.position > 1
        self.has_right2 = self.position < z.subs - 2
        if margin is not None:
            self.lend(margin)

    def lend(self, margin):
        blk = self.z.blk
        self.give_right = pl.multiple_of(margin[0, 0] * blk, blk)
        self.give_left = pl.multiple_of(margin[0, 1] * blk, blk)

    def row_mask(self):
        z = self.z
        rows = lax.broadcasted_iota(jnp.int32, (z.owned, z.loads), 0)
        return rows < self.live

    def kept(self, value):
        z = self.z
        low = value[z.owned : z.owned + z.blk]
        high = value[z.owned + z.blk :]
        return jnp.concatenate(
            [
                jnp.where(self.row_mask(), value[: z.owned], 0.0),
                jnp.where(self.has_left, low, 0.0),
                jnp.where(self.has_right, high, 0.0),
            ],
            axis=0,
        )

    def right_block(self, ref):
        return ref[pl.ds(self.give_right, self.z.blk), :]

    def left_block(self, ref):
        return ref[pl.ds(self.give_left, self.z.blk), :]

    def ahead(self, ref):
        z = self.z
        return jnp.concatenate([ref[z.owned + z.blk :, :], self.right_block(ref)], axis=0)

    def behind(self, ref):
        z = self.z
        return jnp.concatenate([ref[z.owned : z.owned + z.blk, :], self.left_block(ref)], axis=0)

    def pair(self, ahead, behind):
        return jnp.where(self.even, ahead, behind), jnp.where(self.even, behind, ahead)

    def sides(self, first, second):
        return jnp.where(self.even, second, first), jnp.where(self.even, first, second)

    def add_lent(self, target, scale, from_left, from_right, source=None):
        z = self.z
        source = target if source is None else source
        for spot, value in (
            (slice(z.owned, z.owned + z.blk), from_left[z.blk :]),
            (slice(z.owned + z.blk, z.order), from_right[z.blk :]),
            (pl.ds(self.give_left, z.blk), from_left[: z.blk]),
            (pl.ds(self.give_right, z.blk), from_right[: z.blk]),
        ):
            target[spot, :] = source[spot, :] + (value if scale == 1.0 else scale * value)


def selection(z, first, second):
    row = lax.broadcasted_iota(jnp.int32, (z.order, z.side), 0)
    col = lax.broadcasted_iota(jnp.int32, (z.order, z.side), 1)
    return (row == jnp.where(col < z.blk, first + col, second - z.blk + col)).astype(BF16)


def start_all(sem, *pairs):
    copies = [
        pltpu.make_async_copy(source, target, sem.at[k])
        for k, (source, target) in enumerate(pairs)
    ]
    for copy in copies:
        copy.start()
    return copies


def first_kernel(
    z, live, source_far, vectors_far, panel_far, margin_far, slots, own, lent, *scratch
):
    source, vectors_t, panel, margin, sem = scratch
    loads = start_all(
        sem,
        (margin_far, margin),
        (vectors_far, vectors_t),
        (panel_far, panel),
        (source_far, source),
    )
    loads[0].wait()
    at = Place(z, live, margin)
    loads[1].wait()
    rows = selection(z, z.owned + z.blk, at.give_right)
    ahead_vectors = mm(vectors_t[...], rows).astype(BF16)
    rows = selection(z, z.owned, at.give_left)
    behind_vectors = mm(vectors_t[...], rows).astype(BF16)
    lent[...] = jnp.concatenate([ahead_vectors, behind_vectors], axis=0)
    loads[2].wait()
    loads[3].wait()
    own[...] = jnp.where(at.row_mask(), source[...], 0.0)
    ahead = jnp.concatenate([ahead_vectors, at.right_block(own).astype(BF16)], axis=0)
    behind = jnp.concatenate([behind_vectors, at.left_block(own).astype(BF16)], axis=0)
    for k in range(z.subs):
        first = min(max(k - 2, 0), z.subs - z.near) * z.modes
        for chunk in range(z.chunks):
            slots[k, chunk * z.window : (chunk + 1) * z.window, :] = panel[
                chunk, first : first + z.window, :
            ]
        slots[k, z.wide :, :] = jnp.where(k > at.position, ahead, behind)


def static_kernel(z, live, operator_far, inverse_far, margin_far, vectors_t, *refs):
    stack, columns, lifted, first, second, operator, inverse, margin, sem = refs
    loads = start_all(
        sem, (margin_far, margin), (operator_far, operator), (inverse_far, inverse)
    )
    loads[0].wait()
    at = Place(z, live, margin)
    side, modes, picked = z.side, z.modes, z.picked
    from_left = selection(z, at.give_left, z.owned)
    from_right = selection(z, at.give_right, z.owned + z.blk)
    col = lax.broadcasted_iota(jnp.int32, (modes, z.order), 1)
    limit = jnp.where(at.has_left, z.owned + z.blk, z.owned)
    kept = (col < at.live) | ((col >= z.owned) & (col < limit))
    kept = jnp.where(kept | ((col >= z.owned + z.blk) & at.has_right), 1.0, 0.0)
    stack[:modes, :] = vectors_t[...]
    masked = (vectors_t[...].astype(F32) * kept).astype(BF16)
    loads[1].wait()
    rows = jnp.concatenate([at.ahead(operator), at.behind(operator)], axis=0)
    columns[:, :side] = mm(operator[...], from_left).astype(BF16)
    columns[:, side:] = mm(operator[...], from_right).astype(BF16)
    up = nt(masked, rows).astype(BF16)
    ahead = at.ahead(columns)
    behind = at.behind(columns)
    ahead = jnp.concatenate([ahead[:, :side], ahead[:, side:], up[:, :side]], axis=0)
    behind = jnp.concatenate([behind[:, side:], behind[:, :side], up[:, side:]], axis=0)
    first[...], second[...] = at.pair(ahead, behind)
    lifted[...] = nt(masked, operator[...]).astype(BF16)
    loads[2].wait()
    stack[modes : modes + picked, :] = jnp.concatenate(
        [at.ahead(inverse), at.behind(inverse)], axis=0
    )
    rows = (rows.astype(F32) * kept[:1]).astype(BF16)
    stack[modes + picked :, :] = mm(rows, inverse[...]).astype(BF16)


def send(z, at, value, momentum, copies, every_out, sem, first, second, far):
    side, modes = z.side, z.modes
    mine = value[:modes].astype(BF16)

    def put(k, carry):
        copies[k] = mine
        return carry

    lax.fori_loop(0, z.subs * z.groups, put, 0, unroll=8)
    copy = pltpu.make_async_copy(copies, every_out, sem)
    copy.start()
    pieces = [value[modes + k * side : modes + (k + 1) * side] for k in range(4)]
    if momentum is not None:
        pieces[2] = pieces[2] + momentum[0]
        pieces[3] = pieces[3] + momentum[1]
    pieces = [piece.astype(BF16) for piece in pieces]
    first[:side, :], second[:side, :] = at.pair(pieces[0], pieces[1])
    first[side:, :], second[side:, :] = at.pair(pieces[2], pieces[3])
    if z.folded:
        far[0][...] = jnp.where(at.has_right2, pieces[0], pieces[1])
    else:
        far[0][...], far[1][...] = pieces[0], pieces[1]
    return copy


def second_kernel(z, live, slots, own, stack, resid, every_out, first, second, *rest):
    far, (copies, sem) = rest[:-2], rest[-2:]
    at = Place(z, live)
    left = slots[jnp.maximum(at.position - 1, 0), z.wide + z.modes :, :]
    right = slots[jnp.minimum(at.position + 1, z.subs - 1), z.wide + z.modes :, :]
    value = jnp.concatenate(
        [
            own[...],
            jnp.where(at.has_left, left.astype(F32), 0.0),
            jnp.where(at.has_right, right.astype(F32), 0.0),
        ],
        axis=0,
    )
    resid[...] = value
    value = mm(stack[...], value.astype(BF16))
    send(z, at, value, None, copies, every_out, sem, first, second, far).wait()


def window_kernel(z, turn, live, resid, inverse_far, operator_far, *refs):
    if turn:
        part_in, coarse, stack, *refs = refs
        if turn > 1:
            solution_far, *refs = refs
        part, product, solution_out, *refs = refs
        inverse, operator, direction, solution, sem = refs
        more = [(solution_far, solution)] if turn > 1 else []
    else:
        slots, lent, lifted, first_static, second_static, *refs = refs
        part, product, spread, panels, inverse, operator, sem = refs
        more = []
    loads = start_all(sem, (inverse_far, inverse), (operator_far, operator), *more)
    at = Place(z, live)
    if turn:
        index = at.position - z.base(at.position)
        own = coarse[pl.ds(pl.multiple_of(index * z.modes, z.modes), z.modes), :]
        direction[...] = part_in[...] + at.kept(tn(stack[: z.modes, :], own))
        step = STEP_SIZES[turn - 1] * direction[: z.owned, :]
        if turn > 1:
            loads[2].wait()
            step = solution[...] + step
        solution[...] = step
        store = pltpu.make_async_copy(solution, solution_out, sem.at[3])
        store.start()
    else:
        for k in range(z.subs):
            for chunk in range(z.chunks):
                start = (k * z.chunks + chunk) * z.loads
                panels[:, start : start + z.loads] = slots[
                    k, chunk * z.window : (chunk + 1) * z.window, :
                ]
        spread_corrections(z, at, slots, lent, lifted, first_static, second_static, spread)
    loads[0].wait()
    value = at.kept(mm(inverse[...], resid[...].astype(BF16)))
    if turn:
        value = value + MOMENTUM[turn] * direction[...]
    part[...] = value
    loads[1].wait()
    product[...] = mm(operator[...], value.astype(BF16))
    if turn:
        store.wait()


def spread_corrections(z, at, slots, lent, lifted, first_static, second_static, spread):
    side, modes = z.side, z.modes
    row = lax.broadcasted_iota(jnp.int32, (modes, 2 * z.window), 0)
    col = lax.broadcasted_iota(jnp.int32, (modes, 2 * z.window), 1)
    base = z.base(at.position)

    def theirs(offset):
        index = jnp.clip(at.position + offset, 0, z.subs - 1)
        return slots[index, z.wide : z.wide + modes, :]

    left, right = at.sides(first_static[2 * side :, :], second_static[2 * side :, :])
    halves = (
        [
            (theirs(-1), -1, at.has_left),
            (theirs(1), 1, at.has_right),
            (theirs(-2), -2, at.has_left2),
            (theirs(2), 2, at.has_right2),
            (lent[:modes, :], 0, True),
            (lent[modes:, :], 0, True),
        ],
        [(left, -1, at.has_left), (right, 1, at.has_right)]
        + [(lifted[:, k : k + side], 0, True) for k in range(0, z.order, side)],
    )
    for segment in range(z.segments):
        total = jnp.zeros((side, 2 * z.window), F32)
        for half, entries in enumerate(halves):
            if segment < len(entries):
                transposed, offset, have = entries[segment]
                first = half * z.window + (at.position + offset - base) * modes
                place = jnp.where(have, 1.0, 0.0) * jnp.where(col == first + row, 1.0, 0.0)
                total = total + tn(transposed, place.astype(BF16))
        spread[segment * side : (segment + 1) * side, :] = total.astype(BF16)


def main_kernel(z, turn, live, *refs):
    last = turn == ITERS - 1
    every, panels, spread, columns, margin_far, product, resid_in, *refs = refs
    first_in, second_in, first_got, second_got, *refs = refs
    far_left, far_right, first_static, second_static, *refs = refs
    if last:
        part, stack, solution_far, solution_out, resid_out, *refs = refs
        margin, error, resid, direction, solution, sem = refs
        loads = start_all(sem, (margin_far, margin), (solution_far, solution))
    else:
        part, stack, resid, every_out, first, second, *refs = refs
        far, (coarse_out, part_out, margin, error, copies, sem) = refs[:-6], refs[-6:]
        loads = start_all(sem, (margin_far, margin))
    at = Place(z, live)
    side, owned, modes = z.side, z.owned, z.modes

    coarse = jnp.zeros((z.window, z.loads), F32)
    for start in range(0, panels.shape[1], 4 * z.loads):
        stop = min(start + 4 * z.loads, panels.shape[1])
        coarse = coarse + mm(panels[:, start:stop], every[start:stop, :])
    coarse = coarse.astype(BF16)
    nothing = jnp.zeros_like(coarse)
    twice = jnp.concatenate(
        [jnp.concatenate([coarse, nothing], axis=1), jnp.concatenate([nothing, coarse], axis=1)],
        axis=0,
    )
    taken = mm(spread[...], twice)

    def term(segment):
        return taken[segment * side : (segment + 1) * side, : z.loads]

    def other_term(start, rows):
        return taken[start : start + rows, z.loads :]

    left_got, right_got = at.sides(first_got[...], second_got[...])
    ahead_in, behind_in = at.pair(first_in[:side, :], second_in[:side, :])
    left_static, right_static = at.sides(first_static[: 2 * side, :], second_static[: 2 * side, :])

    def masked(have, value):
        return jnp.where(have, value.astype(F32), 0.0)

    from_left = masked(at.has_left, left_got[:side]) + term(0)
    from_right = masked(at.has_right, right_got[:side]) + term(1)
    halo = jnp.concatenate([from_left, from_right], axis=0)
    from_left2 = masked(at.has_left2, far_left[...]) + term(2)
    from_right2 = masked(at.has_right2, far_right[...]) + term(3)
    loads[0].wait()
    at.lend(margin)
    to_right = (ahead_in.astype(F32) + term(4)).astype(BF16)
    to_left = (behind_in.astype(F32) + term(5)).astype(BF16)
    if last:
        index = at.position - z.base(at.position)
        error[: z.window, :] = coarse.astype(F32)
        own = error[pl.ds(pl.multiple_of(index * modes, modes), modes), :].astype(BF16)
        direction[...] = part[...] + at.kept(tn(stack[:modes, :], own))
        at.add_lent(direction, 1.0, from_left, from_right)
        loads[1].wait()
        solution[...] = solution[...] + STEP_SIZES[turn] * direction[:owned, :]
        store_solution = pltpu.make_async_copy(solution, solution_out, sem.at[2])
        store_solution.start()

    def borrowed(have, got, statics, far, near, start):
        rows = jnp.concatenate([statics[:side], statics[side:]], axis=1)
        value = mm(rows, jnp.concatenate([far.astype(BF16), near], axis=0))
        return masked(have, value + got[side:].astype(F32)) + other_term(start, side)

    applied = product[...] + other_term(2 * side, z.order) + mm(columns[...], halo.astype(BF16))
    left = borrowed(at.has_left, left_got, left_static, from_left2, to_left, 0)
    right = borrowed(at.has_right, right_got, right_static, from_right2, to_right, side)
    error[...] = applied
    resid[...] = resid_in[...] - STEP_SIZES[turn] * at.kept(applied)
    at.add_lent(resid, -STEP_SIZES[turn], left, right)
    if last:
        store = pltpu.make_async_copy(resid.at[pl.ds(0, owned), :], resid_out, sem.at[3])
        store.start()
        store.wait()
        store_solution.wait()
    else:
        value = mm(stack[...], resid[...].astype(BF16))
        beta = MOMENTUM[turn + 1]
        momentum = beta * at.ahead(error), beta * at.behind(error)
        store = send(z, at, value, momentum, copies, every_out, sem.at[2], first, second, far)
        coarse_out[...] = coarse
        at.add_lent(part_out, 1.0, from_left, from_right, part)
        store.wait()


def body(
    right_side, live_rows, margin_blocks, local_operator, local_inverse, deflation, coarse_inverse
):
    z = Sizes(right_side, deflation, coarse_inverse)
    source = right_side[0, 0]
    operator = Far(local_operator[0, 0])
    inverse = Far(local_inverse[0, 0])
    vectors_t = deflation[0, 0].T
    margin = Far(margin_blocks.reshape(1, -1))
    scalars = (live_rows,)
    owned, order, loads, modes, side = z.owned, z.order, z.loads, z.modes, z.side
    devices = z.subs * z.groups

    pick = pltpu.SMEM((1, margin_blocks.shape[-1]), jnp.int32)
    sems = pltpu.SemaphoreType.DMA
    square = pltpu.VMEM((order, order), BF16)

    def part(function, *more):
        return functools.partial(function, z, *more)

    def low(*dims):
        return shape(*dims, dtype=BF16)

    def pairs(first):
        partner = list(range(z.subs))
        for k in range(first, z.subs - 1, 2):
            partner[k], partner[k + 1] = k + 1, k
        return list(enumerate(partner))

    def exchange(first, second):
        return lax.ppermute(second, "sub", pairs(1)), lax.ppermute(first, "sub", pairs(0))

    def ring(offset):
        return [(i, (i + offset) % z.subs) for i in range(z.subs)]

    panel = coarse_inverse.reshape(-1, z.chunks, loads).swapaxes(0, 1)
    slots, own, lent = run(
        part(first_kernel),
        "first",
        [
            low(z.subs, z.wide + modes + z.blk, loads),
            shape(owned, loads),
            low(2 * modes, side),
        ],
        [Far(source), Far(vectors_t), Far(panel), margin],
        scalars,
        [
            pltpu.VMEM(source.shape, F32),
            pltpu.VMEM(vectors_t.shape, BF16),
            pltpu.VMEM(panel.shape, BF16),
            pick,
            sems((4,)),
        ],
    )
    slots = lax.all_to_all(slots, "sub", 0, 0, tiled=True)
    stack, columns, lifted, first, second = run(
        part(static_kernel),
        "static",
        [low(z.stack, order), low(order, 2 * side), low(modes, order)]
        + [low(2 * side + modes, loads)] * 2,
        [operator, inverse, margin, vectors_t],
        scalars,
        [square, square, pick, sems((3,))],
    )
    second_static, first_static = exchange(first, second)
    sent = [shape(order, loads), Far(low(devices, modes, loads))]
    sent += [low(2 * side, loads)] * 2 + [low(side, loads)] * (1 if z.folded else 2)
    copies = pltpu.VMEM((devices, modes, loads), BF16)
    resid, every, first, second, *far = run(
        part(second_kernel),
        "second",
        sent,
        [slots, own, stack],
        scalars,
        [copies, sems(())],
    )
    full = shape(order, loads)
    floor = pltpu.VMEM((order, loads), F32)
    solution = None
    for turn in range(ITERS):
        last = turn == ITERS - 1
        every = lax.all_to_all(every, ("sub", "grp"), 0, 0, tiled=True)
        every = every.reshape(devices * modes, loads)
        second_got, first_got = exchange(first, second)
        if z.folded:
            far_left = far_right = lax.ppermute(far[0], "sub", ring(2))
        else:
            far_left = lax.ppermute(far[0], "sub", ring(2))
            far_right = lax.ppermute(far[1], "sub", ring(-2))
        args = [resid, inverse, operator]
        if turn:
            args += [error, coarse, stack]
            args += [solution] if turn > 1 else []
            outs = [full, full, Far(shape(owned, loads))]
            work = [square, square, floor, pltpu.VMEM((owned, loads), F32), sems((4,))]
        else:
            args += [slots, lent, lifted, first_static, second_static]
            outs = [full, full, low(z.segments * side, 2 * z.window)]
            outs += [low(z.window, z.subs * z.chunks * loads)]
            work = [square, square, sems((2,))]
        error, product, *more = run(
            part(window_kernel, turn),
            f"window{turn}",
            outs,
            args,
            scalars,
            work,
            aliases={len(scalars) + 3: 0} if turn else None,
        )
        if turn:
            solution = Far(more[0])
        else:
            spread, panels = more
        args = [every, panels, spread, columns, margin, product, resid]
        args += [first, second, first_got, second_got, far_left, far_right]
        args += [first_static, second_static]
        if last:
            solution, resid = run(
                part(main_kernel, turn),
                f"main{turn}",
                [Far(shape(owned, loads))] * 2,
                args + [error, stack, solution],
                scalars,
                [pick, floor, floor, floor, pltpu.VMEM((owned, loads), F32), sems((4,))],
            )
        else:
            outs = sent + [low(z.window, loads), full]
            resid, every, first, second, *far, coarse, error = run(
                part(main_kernel, turn),
                f"main{turn}",
                outs,
                args + [error, stack],
                scalars,
                [pick, floor, copies, sems((3,))],
                aliases={len(scalars) + len(args): len(outs) - 1},
            )
    return (solution[None, None], resid[None, None])


def solution(mesh):
    return jax.shard_map(
        body,
        mesh=mesh,
        in_specs=(
            P("grp", "sub", None, None),
            P("grp", "sub"),
            P("grp", "sub", None),
            P("grp", "sub", None, None),
            P("grp", "sub", None, None),
            P("grp", "sub", None, None),
            P("grp", "sub"),
        ),
        out_specs=(P("grp", "sub", None, None), P("grp", "sub", None, None)),
        check_vma=False,
    )
```

```python
import functools

import jax
import jax.numpy as jnp
from jax import lax
from jax.experimental import pallas as pl
from jax.experimental.pallas import tpu as pltpu
from jax.sharding import PartitionSpec as P

ITERS = 3


STEP_SIZES = (0.8, 0.9, 1.0)
MOMENTUM = (0.0, 0.3, 0.3)

F32 = jnp.float32
BF16 = jnp.bfloat16


def mm(a, b):
    return jnp.dot(a, b, preferred_element_type=F32)


def tn(a, b):
    return lax.dot_general(a, b, (((0,), (0,)), ((), ())), preferred_element_type=F32)


def nt(a, b):
    return lax.dot_general(a, b, (((1,), (1,)), ((), ())), preferred_element_type=F32)


def run(kernel, outs, args, scalars=(), scratch=(), flops=1 << 22, aliases=None):
    nbytes = sum(x.size * x.dtype.itemsize for x in map(bare, [*args, *outs]))
    return pl.pallas_call(
        kernel,
        out_shape=[held(x) for x in outs],
        in_specs=[pl.BlockSpec(memory_space=pltpu.SMEM)] * len(scalars) + [spec(x) for x in args],
        out_specs=[spec(x) for x in outs],
        scratch_shapes=list(scratch),
        input_output_aliases=aliases or {},
        compiler_params=pltpu.CompilerParams(vmem_limit_bytes=24 << 20),
        cost_estimate=pl.CostEstimate(flops=flops, bytes_accessed=nbytes, transcendentals=0),
    )(
        *scalars,
        *map(given, args),
    )


class Far:
    def __init__(self, array):
        self.array = array


def bare(x):
    return x.array if isinstance(x, Far) else x


def held(x):
    return pltpu.HBM(x.array.shape, x.array.dtype) if isinstance(x, Far) else x


def given(x):
    return pltpu.with_memory_space_constraint(x.array, pltpu.HBM) if isinstance(x, Far) else x


def spec(x):
    return pl.BlockSpec(memory_space=pltpu.HBM if isinstance(x, Far) else pltpu.VMEM)


def shape(*dims, dtype=F32):
    return jax.ShapeDtypeStruct(dims, dtype)


class Sizes:
    def __init__(self, right_side, deflation, coarse_inverse):
        self.owned, self.loads = right_side.shape[-2:]
        self.order, self.modes = deflation.shape[-2:]
        self.blk = (self.order - self.owned) // 2
        self.side = 2 * self.blk
        self.subs = lax.axis_size("sub")
        self.groups = lax.axis_size("grp")
        self.near = min(self.subs, 5)
        self.chunks = coarse_inverse.shape[1] // self.loads
        self.window = self.near * self.modes
        self.wide = self.window * self.chunks
        self.picked = 2 * self.side
        self.stack = self.modes + 2 * self.picked
        self.folded = self.subs == 4
        self.segments = max(6, 2 + self.order // self.side)

    def base(self, position):
        return jnp.clip(position - 2, 0, self.subs - self.near)


class Place:
    def __init__(self, z, live, margin=None):
        self.z = z
        self.position = lax.axis_index("sub")
        self.live = live[0, 0]
        self.has_left = self.position > 0
        self.has_right = self.position < z.subs - 1
        self.has_left2 = self.position > 1
        self.has_right2 = self.position < z.subs - 2
        if margin is not None:
            self.lend(margin)

    def lend(self, margin):
        blk = self.z.blk
        self.give_right = pl.multiple_of(margin[0, 0] * blk, blk)
        self.give_left = pl.multiple_of(margin[0, 1] * blk, blk)

    def row_mask(self):
        z = self.z
        rows = lax.broadcasted_iota(jnp.int32, (z.owned, z.loads), 0)
        return rows < self.live

    def kept(self, value):
        z = self.z
        low = value[z.owned : z.owned + z.blk]
        high = value[z.owned + z.blk :]
        return jnp.concatenate(
            [
                jnp.where(self.row_mask(), value[: z.owned], 0.0),
                jnp.where(self.has_left, low, 0.0),
                jnp.where(self.has_right, high, 0.0),
            ],
            axis=0,
        )

    def right_block(self, ref):
        return ref[pl.ds(self.give_right, self.z.blk), :]

    def left_block(self, ref):
        return ref[pl.ds(self.give_left, self.z.blk), :]

    def ahead(self, ref):
        z = self.z
        return jnp.concatenate([ref[z.owned + z.blk :, :], self.right_block(ref)], axis=0)

    def behind(self, ref):
        z = self.z
        return jnp.concatenate([ref[z.owned : z.owned + z.blk, :], self.left_block(ref)], axis=0)

    def add_lent(self, target, scale, from_left, from_right, source=None):
        z = self.z
        source = target if source is None else source
        for spot, value in (
            (slice(z.owned, z.owned + z.blk), from_left[z.blk :]),
            (slice(z.owned + z.blk, z.order), from_right[z.blk :]),
            (pl.ds(self.give_left, z.blk), from_left[: z.blk]),
            (pl.ds(self.give_right, z.blk), from_right[: z.blk]),
        ):
            target[spot, :] = source[spot, :] + (value if scale == 1.0 else scale * value)


def selection(z, first, second):
    row = lax.broadcasted_iota(jnp.int32, (z.order, z.side), 0)
    col = lax.broadcasted_iota(jnp.int32, (z.order, z.side), 1)
    return (row == jnp.where(col < z.blk, first + col, second - z.blk + col)).astype(BF16)


def start_all(sem, *pairs):
    copies = [
        pltpu.make_async_copy(source, target, sem.at[k])
        for k, (source, target) in enumerate(pairs)
    ]
    for copy in copies:
        copy.start()
    return copies


def first_kernel(
    z, live, source_far, vectors_far, panel_far, margin_far, slots, own, lent, *scratch
):
    source, vectors_t, panel, margin, sem = scratch
    loads = start_all(
        sem,
        (margin_far, margin),
        (vectors_far, vectors_t),
        (panel_far, panel),
        (source_far, source),
    )
    loads[0].wait()
    at = Place(z, live, margin)
    loads[1].wait()
    rows = selection(z, z.owned + z.blk, at.give_right)
    ahead_vectors = mm(vectors_t[...], rows).astype(BF16)
    rows = selection(z, z.owned, at.give_left)
    behind_vectors = mm(vectors_t[...], rows).astype(BF16)
    lent[...] = jnp.concatenate([ahead_vectors, behind_vectors], axis=0)
    loads[2].wait()
    loads[3].wait()
    own[...] = jnp.where(at.row_mask(), source[...], 0.0)
    ahead = jnp.concatenate([ahead_vectors, at.right_block(own).astype(BF16)], axis=0)
    behind = jnp.concatenate([behind_vectors, at.left_block(own).astype(BF16)], axis=0)
    for k in range(z.subs):
        first = min(max(k - 2, 0), z.subs - z.near) * z.modes
        for chunk in range(z.chunks):
            slots[k, chunk * z.window : (chunk + 1) * z.window, :] = panel[
                chunk, first : first + z.window, :
            ]
        slots[k, z.wide :, :] = jnp.where(k > at.position, ahead, behind)


def static_kernel(z, live, operator_far, inverse_far, margin_far, vectors_t, *refs):
    stack, columns, lifted, first, second, operator, inverse, margin, sem = refs
    loads = start_all(
        sem, (margin_far, margin), (operator_far, operator), (inverse_far, inverse)
    )
    loads[0].wait()
    at = Place(z, live, margin)
    side, modes, picked = z.side, z.modes, z.picked
    from_left = selection(z, at.give_left, z.owned)
    from_right = selection(z, at.give_right, z.owned + z.blk)
    col = lax.broadcasted_iota(jnp.int32, (modes, z.order), 1)
    limit = jnp.where(at.has_left, z.owned + z.blk, z.owned)
    kept = (col < at.live) | ((col >= z.owned) & (col < limit))
    kept = jnp.where(kept | ((col >= z.owned + z.blk) & at.has_right), 1.0, 0.0)
    stack[:modes, :] = vectors_t[...]
    masked = (vectors_t[...].astype(F32) * kept).astype(BF16)
    loads[1].wait()
    rows = jnp.concatenate([at.ahead(operator), at.behind(operator)], axis=0)
    columns[:, :side] = mm(operator[...], from_left).astype(BF16)
    columns[:, side:] = mm(operator[...], from_right).astype(BF16)
    up = nt(masked, rows).astype(BF16)
    ahead = at.ahead(columns)
    behind = at.behind(columns)
    ahead = jnp.concatenate([ahead[:, :side], ahead[:, side:], up[:, :side]], axis=0)
    behind = jnp.concatenate([behind[:, side:], behind[:, :side], up[:, side:]], axis=0)
    first[...], second[...] = ahead, behind
    lifted[...] = nt(masked, operator[...]).astype(BF16)
    loads[2].wait()
    stack[modes : modes + picked, :] = jnp.concatenate(
        [at.ahead(inverse), at.behind(inverse)], axis=0
    )
    rows = (rows.astype(F32) * kept[:1]).astype(BF16)
    stack[modes + picked :, :] = mm(rows, inverse[...]).astype(BF16)


def send(z, at, value, momentum, copies, every_out, sem, first, second, far):
    side, modes = z.side, z.modes
    mine = value[:modes].astype(BF16)

    def put(k, carry):
        copies[k] = mine
        return carry

    lax.fori_loop(0, z.subs * z.groups, put, 0, unroll=8)
    copy = pltpu.make_async_copy(copies, every_out, sem)
    copy.start()
    pieces = [value[modes + k * side : modes + (k + 1) * side] for k in range(4)]
    if momentum is not None:
        pieces[2] = pieces[2] + momentum[0]
        pieces[3] = pieces[3] + momentum[1]
    pieces = [piece.astype(BF16) for piece in pieces]
    first[:side, :], second[:side, :] = pieces[0], pieces[1]
    first[side:, :], second[side:, :] = pieces[2], pieces[3]
    if z.folded:
        far[0][...] = jnp.where(at.has_right2, pieces[0], pieces[1])
    else:
        far[0][...], far[1][...] = pieces[0], pieces[1]
    return copy


def second_kernel(z, live, slots, own, stack, resid, every_out, first, second, *rest):
    far, (copies, sem) = rest[:-2], rest[-2:]
    at = Place(z, live)
    left = slots[jnp.maximum(at.position - 1, 0), z.wide + z.modes :, :]
    right = slots[jnp.minimum(at.position + 1, z.subs - 1), z.wide + z.modes :, :]
    value = jnp.concatenate(
        [
            own[...],
            jnp.where(at.has_left, left.astype(F32), 0.0),
            jnp.where(at.has_right, right.astype(F32), 0.0),
        ],
        axis=0,
    )
    resid[...] = value
    value = mm(stack[...], value.astype(BF16))
    send(z, at, value, None, copies, every_out, sem, first, second, far).wait()


def window_kernel(z, turn, live, resid, inverse_far, operator_far, *refs):
    if turn:
        part_in, coarse, stack, *refs = refs
        if turn > 1:
            solution_far, *refs = refs
        part, product, solution_out, *refs = refs
        inverse, operator, direction, solution, sem = refs
        more = [(solution_far, solution)] if turn > 1 else []
    else:
        slots, lent, lifted, left_static, right_static, *refs = refs
        part, product, spread, panels, inverse, operator, sem = refs
        more = []
    loads = start_all(sem, (inverse_far, inverse), (operator_far, operator), *more)
    at = Place(z, live)
    if turn:
        index = at.position - z.base(at.position)
        own = coarse[pl.ds(pl.multiple_of(index * z.modes, z.modes), z.modes), :]
        direction[...] = part_in[...] + at.kept(tn(stack[: z.modes, :], own))
        step = STEP_SIZES[turn - 1] * direction[: z.owned, :]
        if turn > 1:
            loads[2].wait()
            step = solution[...] + step
        solution[...] = step
        store = pltpu.make_async_copy(solution, solution_out, sem.at[3])
        store.start()
    else:
        for k in range(z.subs):
            for chunk in range(z.chunks):
                start = (k * z.chunks + chunk) * z.loads
                panels[:, start : start + z.loads] = slots[
                    k, chunk * z.window : (chunk + 1) * z.window, :
                ]
        spread_corrections(z, at, slots, lent, lifted, left_static, right_static, spread)
    loads[0].wait()
    value = at.kept(mm(inverse[...], resid[...].astype(BF16)))
    if turn:
        value = value + MOMENTUM[turn] * direction[...]
    part[...] = value
    loads[1].wait()
    product[...] = mm(operator[...], value.astype(BF16))
    if turn:
        store.wait()


def spread_corrections(z, at, slots, lent, lifted, left_static, right_static, spread):
    side, modes = z.side, z.modes
    row = lax.broadcasted_iota(jnp.int32, (modes, 2 * z.window), 0)
    col = lax.broadcasted_iota(jnp.int32, (modes, 2 * z.window), 1)
    base = z.base(at.position)

    def theirs(offset):
        index = jnp.clip(at.position + offset, 0, z.subs - 1)
        return slots[index, z.wide : z.wide + modes, :]

    left, right = left_static[2 * side :, :], right_static[2 * side :, :]
    halves = (
        [
            (theirs(-1), -1, at.has_left),
            (theirs(1), 1, at.has_right),
            (theirs(-2), -2, at.has_left2),
            (theirs(2), 2, at.has_right2),
            (lent[:modes, :], 0, True),
            (lent[modes:, :], 0, True),
        ],
        [(left, -1, at.has_left), (right, 1, at.has_right)]
        + [(lifted[:, k : k + side], 0, True) for k in range(0, z.order, side)],
    )
    for segment in range(z.segments):
        total = jnp.zeros((side, 2 * z.window), F32)
        for half, entries in enumerate(halves):
            if segment < len(entries):
                transposed, offset, have = entries[segment]
                first = half * z.window + (at.position + offset - base) * modes
                place = jnp.where(have, 1.0, 0.0) * jnp.where(col == first + row, 1.0, 0.0)
                total = total + tn(transposed, place.astype(BF16))
        spread[segment * side : (segment + 1) * side, :] = total.astype(BF16)


def main_kernel(z, turn, live, *refs):
    last = turn == ITERS - 1
    every, panels, spread, columns, margin_far, product, resid_in, *refs = refs
    ahead_in, behind_in, left_got, right_got, *refs = refs
    far_left, far_right, left_static, right_static, *refs = refs
    if last:
        part, stack, solution_far, solution_out, resid_out, *refs = refs
        margin, error, resid, direction, solution, sem = refs
        loads = start_all(sem, (margin_far, margin), (solution_far, solution))
    else:
        part, stack, resid, every_out, first, second, *refs = refs
        far, (coarse_out, part_out, margin, error, copies, sem) = refs[:-6], refs[-6:]
        loads = start_all(sem, (margin_far, margin))
    at = Place(z, live)
    side, owned, modes = z.side, z.owned, z.modes

    coarse = jnp.zeros((z.window, z.loads), F32)
    for start in range(0, panels.shape[1], 4 * z.loads):
        stop = min(start + 4 * z.loads, panels.shape[1])
        coarse = coarse + mm(panels[:, start:stop], every[start:stop, :])
    coarse = coarse.astype(BF16)
    nothing = jnp.zeros_like(coarse)
    twice = jnp.concatenate(
        [jnp.concatenate([coarse, nothing], axis=1), jnp.concatenate([nothing, coarse], axis=1)],
        axis=0,
    )
    taken = mm(spread[...], twice)

    def term(segment):
        return taken[segment * side : (segment + 1) * side, : z.loads]

    def other_term(start, rows):
        return taken[start : start + rows, z.loads :]


    def masked(have, value):
        return jnp.where(have, value.astype(F32), 0.0)

    from_left = masked(at.has_left, left_got[:side, :]) + term(0)
    from_right = masked(at.has_right, right_got[:side, :]) + term(1)
    halo = jnp.concatenate([from_left, from_right], axis=0)
    from_left2 = masked(at.has_left2, far_left[...]) + term(2)
    from_right2 = masked(at.has_right2, far_right[...]) + term(3)
    loads[0].wait()
    at.lend(margin)
    to_right = (ahead_in[:side, :].astype(F32) + term(4)).astype(BF16)
    to_left = (behind_in[:side, :].astype(F32) + term(5)).astype(BF16)
    if last:
        index = at.position - z.base(at.position)
        error[: z.window, :] = coarse.astype(F32)
        own = error[pl.ds(pl.multiple_of(index * modes, modes), modes), :].astype(BF16)
        direction[...] = part[...] + at.kept(tn(stack[:modes, :], own))
        at.add_lent(direction, 1.0, from_left, from_right)
        loads[1].wait()
        solution[...] = solution[...] + STEP_SIZES[turn] * direction[:owned, :]
        store_solution = pltpu.make_async_copy(solution, solution_out, sem.at[2])
        store_solution.start()

    def borrowed(have, got, statics, far, near, start):
        rows = jnp.concatenate([statics[:side, :], statics[side : 2 * side, :]], axis=1)
        value = mm(rows, jnp.concatenate([far.astype(BF16), near], axis=0))
        return masked(have, value + got[side:, :].astype(F32)) + other_term(start, side)

    applied = product[...] + other_term(2 * side, z.order) + mm(columns[...], halo.astype(BF16))
    left = borrowed(at.has_left, left_got, left_static, from_left2, to_left, 0)
    right = borrowed(at.has_right, right_got, right_static, from_right2, to_right, side)
    error[...] = applied
    resid[...] = resid_in[...] - STEP_SIZES[turn] * at.kept(applied)
    at.add_lent(resid, -STEP_SIZES[turn], left, right)
    if last:
        store = pltpu.make_async_copy(resid.at[pl.ds(0, owned), :], resid_out, sem.at[3])
        store.start()
        store.wait()
        store_solution.wait()
    else:
        value = mm(stack[...], resid[...].astype(BF16))
        beta = MOMENTUM[turn + 1]
        momentum = beta * at.ahead(error), beta * at.behind(error)
        store = send(z, at, value, momentum, copies, every_out, sem.at[2], first, second, far)
        coarse_out[...] = coarse
        at.add_lent(part_out, 1.0, from_left, from_right, part)
        store.wait()


def body(
    right_side, live_rows, margin_blocks, local_operator, local_inverse, deflation, coarse_inverse
):
    z = Sizes(right_side, deflation, coarse_inverse)
    source = right_side[0, 0]
    operator = Far(local_operator[0, 0])
    inverse = Far(local_inverse[0, 0])
    vectors_t = deflation[0, 0].T
    margin = Far(margin_blocks.reshape(1, -1))
    scalars = (live_rows,)
    owned, order, loads, modes, side = z.owned, z.order, z.loads, z.modes, z.side
    devices = z.subs * z.groups

    pick = pltpu.SMEM((1, margin_blocks.shape[-1]), jnp.int32)
    sems = pltpu.SemaphoreType.DMA
    square = pltpu.VMEM((order, order), BF16)

    def part(function, *more):
        return functools.partial(function, z, *more)

    def low(*dims):
        return shape(*dims, dtype=BF16)

    def exchange(first, second):
        return lax.ppermute(first, "sub", ring(1)), lax.ppermute(second, "sub", ring(-1))

    def ring(offset):
        return [(i, (i + offset) % z.subs) for i in range(z.subs)]

    panel = coarse_inverse.reshape(-1, z.chunks, loads).swapaxes(0, 1)
    slots, own, lent = run(
        part(first_kernel),
        [
            low(z.subs, z.wide + modes + z.blk, loads),
            shape(owned, loads),
            low(2 * modes, side),
        ],
        [Far(source), Far(vectors_t), Far(panel), margin],
        scalars,
        [
            pltpu.VMEM(source.shape, F32),
            pltpu.VMEM(vectors_t.shape, BF16),
            pltpu.VMEM(panel.shape, BF16),
            pick,
            sems((4,)),
        ],
    )
    slots = lax.all_to_all(slots, "sub", 0, 0, tiled=True)
    stack, columns, lifted, first, second = run(
        part(static_kernel),
        [low(z.stack, order), low(order, 2 * side), low(modes, order)]
        + [low(2 * side + modes, loads)] * 2,
        [operator, inverse, margin, vectors_t],
        scalars,
        [square, square, pick, sems((3,))],
    )
    left_static, right_static = exchange(first, second)
    sent = [shape(order, loads), Far(low(devices, modes, loads))]
    sent += [low(2 * side, loads)] * 2 + [low(side, loads)] * (1 if z.folded else 2)
    copies = pltpu.VMEM((devices, modes, loads), BF16)
    resid, every, first, second, *far = run(
        part(second_kernel), sent, [slots, own, stack], scalars, [copies, sems(())]
    )
    full = shape(order, loads)
    floor = pltpu.VMEM((order, loads), F32)
    solution = None
    for turn in range(ITERS):
        last = turn == ITERS - 1
        every = lax.all_to_all(every, ("sub", "grp"), 0, 0, tiled=True)
        every = every.reshape(devices * modes, loads)
        left_got, right_got = exchange(first, second)
        if z.folded:
            far_left = far_right = lax.ppermute(far[0], "sub", ring(2))
        else:
            far_left = lax.ppermute(far[0], "sub", ring(2))
            far_right = lax.ppermute(far[1], "sub", ring(-2))
        args = [resid, inverse, operator]
        if turn:
            args += [error, coarse, stack]
            args += [solution] if turn > 1 else []
            outs = [full, full, Far(shape(owned, loads))]
            work = [square, square, floor, pltpu.VMEM((owned, loads), F32), sems((4,))]
        else:
            args += [slots, lent, lifted, left_static, right_static]
            outs = [full, full, low(z.segments * side, 2 * z.window)]
            outs += [low(z.window, z.subs * z.chunks * loads)]
            work = [square, square, sems((2,))]
        error, product, *more = run(
            part(window_kernel, turn),
            outs,
            args,
            scalars,
            work,
            aliases={len(scalars) + 3: 0} if turn else None,
        )
        if turn:
            solution = Far(more[0])
        else:
            spread, panels = more
        args = [every, panels, spread, columns, margin, product, resid]
        args += [first, second, left_got, right_got, far_left, far_right]
        args += [left_static, right_static]
        if last:
            solution, resid = run(
                part(main_kernel, turn),
                [Far(shape(owned, loads))] * 2,
                args + [error, stack, solution],
                scalars,
                [pick, floor, floor, floor, pltpu.VMEM((owned, loads), F32), sems((4,))],
            )
        else:
            outs = sent + [low(z.window, loads), full]
            resid, every, first, second, *far, coarse, error = run(
                part(main_kernel, turn),
                outs,
                args + [error, stack],
                scalars,
                [pick, floor, copies, sems((3,))],
                aliases={len(scalars) + len(args): len(outs) - 1},
            )
    return (solution[None, None], resid[None, None])


def solution(mesh):
    return jax.shard_map(
        body,
        mesh=mesh,
        in_specs=(
            P("grp", "sub", None, None),
            P("grp", "sub"),
            P("grp", "sub", None),
            P("grp", "sub", None, None),
            P("grp", "sub", None, None),
            P("grp", "sub", None, None),
            P("grp", "sub"),
        ),
        out_specs=(P("grp", "sub", None, None), P("grp", "sub", None, None)),
        check_vma=False,
    )
```

```python
import functools

import jax
import jax.numpy as jnp
from jax import lax
from jax.experimental import pallas as pl
from jax.experimental.pallas import tpu as pltpu
from jax.sharding import PartitionSpec as P

ITERS = 3


STEP_SIZES = (0.8, 0.9, 1.0)
MOMENTUM = (0.0, 0.3, 0.3)

F32 = jnp.float32
BF16 = jnp.bfloat16


def mm(a, b):
    return jnp.dot(a, b, preferred_element_type=F32)


def tn(a, b):
    return lax.dot_general(a, b, (((0,), (0,)), ((), ())), preferred_element_type=F32)


def nt(a, b):
    return lax.dot_general(a, b, (((1,), (1,)), ((), ())), preferred_element_type=F32)


def run(kernel, outs, args, scalars=(), scratch=(), flops=1 << 22, aliases=None):
    nbytes = sum(x.size * x.dtype.itemsize for x in map(bare, [*args, *outs]))
    return pl.pallas_call(
        kernel,
        out_shape=[held(x) for x in outs],
        in_specs=[pl.BlockSpec(memory_space=pltpu.SMEM)] * len(scalars) + [spec(x) for x in args],
        out_specs=[spec(x) for x in outs],
        scratch_shapes=list(scratch),
        input_output_aliases=aliases or {},
        compiler_params=pltpu.CompilerParams(vmem_limit_bytes=24 << 20),
        cost_estimate=pl.CostEstimate(flops=flops, bytes_accessed=nbytes, transcendentals=0),
    )(
        *scalars,
        *map(given, args),
    )


class Far:
    def __init__(self, array):
        self.array = array


def bare(x):
    return x.array if isinstance(x, Far) else x


def held(x):
    return pltpu.HBM(x.array.shape, x.array.dtype) if isinstance(x, Far) else x


def given(x):
    return pltpu.with_memory_space_constraint(x.array, pltpu.HBM) if isinstance(x, Far) else x


def spec(x):
    return pl.BlockSpec(memory_space=pltpu.HBM if isinstance(x, Far) else pltpu.VMEM)


def shape(*dims, dtype=F32):
    return jax.ShapeDtypeStruct(dims, dtype)


class Sizes:
    def __init__(self, right_side, deflation, coarse_inverse):
        self.owned, self.loads = right_side.shape[-2:]
        self.order, self.modes = deflation.shape[-2:]
        self.blk = (self.order - self.owned) // 2
        self.side = 2 * self.blk
        self.subs = lax.axis_size("sub")
        self.groups = lax.axis_size("grp")
        self.near = min(self.subs, 5)
        self.chunks = coarse_inverse.shape[1] // self.loads
        self.window = self.near * self.modes
        self.wide = self.window * self.chunks
        self.picked = 2 * self.side
        self.stack = self.modes + 2 * self.picked
        self.folded = self.subs == 4
        self.segments = max(6, 2 + self.order // self.side)

    def base(self, position):
        return jnp.clip(position - 2, 0, self.subs - self.near)


class Place:
    def __init__(self, z, live, margin=None):
        self.z = z
        self.position = lax.axis_index("sub")
        self.live = None if live is None else live[0, 0]
        self.has_left = self.position > 0
        self.has_right = self.position < z.subs - 1
        self.has_left2 = self.position > 1
        self.has_right2 = self.position < z.subs - 2
        if margin is not None:
            self.lend(margin[0, 0], margin[0, 1])

    def lend(self, right, left):
        blk = self.z.blk
        self.give_right = pl.multiple_of(right * blk, blk)
        self.give_left = pl.multiple_of(left * blk, blk)

    def row_mask(self):
        z = self.z
        rows = lax.broadcasted_iota(jnp.int32, (z.owned, z.loads), 0)
        return rows < self.live

    def kept(self, value):
        z = self.z
        low = value[z.owned : z.owned + z.blk]
        high = value[z.owned + z.blk :]
        return jnp.concatenate(
            [
                jnp.where(self.row_mask(), value[: z.owned], 0.0),
                jnp.where(self.has_left, low, 0.0),
                jnp.where(self.has_right, high, 0.0),
            ],
            axis=0,
        )

    def kept_columns(self):
        z = self.z
        col = lax.broadcasted_iota(jnp.int32, (z.modes, z.order), 1)
        limit = jnp.where(self.has_left, z.owned + z.blk, z.owned)
        kept = (col < self.live) | ((col >= z.owned) & (col < limit))
        return jnp.where(kept | ((col >= z.owned + z.blk) & self.has_right), 1.0, 0.0)

    def lent_columns(self):
        z = self.z
        return jnp.concatenate(
            [
                selection(z, self.give_left, z.owned),
                selection(z, self.give_right, z.owned + z.blk),
            ],
            axis=1,
        )

    def right_block(self, ref):
        return ref[pl.ds(self.give_right, self.z.blk), :]

    def left_block(self, ref):
        return ref[pl.ds(self.give_left, self.z.blk), :]

    def ahead(self, ref):
        z = self.z
        return jnp.concatenate([ref[z.owned + z.blk :, :], self.right_block(ref)], axis=0)

    def behind(self, ref):
        z = self.z
        return jnp.concatenate([ref[z.owned : z.owned + z.blk, :], self.left_block(ref)], axis=0)

    def add_lent(self, target, scale, from_left, from_right, source=None):
        z = self.z
        source = target if source is None else source
        for spot, value in (
            (slice(z.owned, z.owned + z.blk), from_left[z.blk :]),
            (slice(z.owned + z.blk, z.order), from_right[z.blk :]),
            (pl.ds(self.give_left, z.blk), from_left[: z.blk]),
            (pl.ds(self.give_right, z.blk), from_right[: z.blk]),
        ):
            target[spot, :] = source[spot, :] + (value if scale == 1.0 else scale * value)


def selection(z, first, second):
    row = lax.broadcasted_iota(jnp.int32, (z.order, z.side), 0)
    col = lax.broadcasted_iota(jnp.int32, (z.order, z.side), 1)
    return (row == jnp.where(col < z.blk, first + col, second - z.blk + col)).astype(BF16)


def start_all(sem, *pairs):
    copies = [
        pltpu.make_async_copy(source, target, sem.at[k])
        for k, (source, target) in enumerate(pairs)
    ]
    for copy in copies:
        copy.start()
    return copies


def first_kernel(
    z, source_far, vectors_far, panel_far, margin_far, operator_far, inverse_far, *refs
):
    slots_far, lent, spot, operator, inverse, slots, *scratch = refs
    source, vectors_t, panel, margin, sem = scratch
    loads = start_all(
        sem,
        (margin_far, margin),
        (vectors_far, vectors_t),
        (panel_far, panel),
        (source_far, source),
        (margin_far, spot),
        (operator_far, operator),
        (inverse_far, inverse),
    )
    loads[0].wait()
    at = Place(z, None, margin)
    loads[1].wait()
    rows = selection(z, z.owned + z.blk, at.give_right)
    ahead_vectors = mm(vectors_t[...], rows).astype(BF16)
    rows = selection(z, z.owned, at.give_left)
    behind_vectors = mm(vectors_t[...], rows).astype(BF16)
    lent[...] = jnp.concatenate([ahead_vectors, behind_vectors], axis=0)
    loads[2].wait()
    loads[4].wait()
    loads[3].wait()
    ahead = jnp.concatenate([ahead_vectors, at.right_block(source).astype(BF16)], axis=0)
    behind = jnp.concatenate([behind_vectors, at.left_block(source).astype(BF16)], axis=0)
    for k in range(z.subs):
        first = min(max(k - 2, 0), z.subs - z.near) * z.modes
        for chunk in range(z.chunks):
            slots[k, chunk * z.window : (chunk + 1) * z.window, :] = panel[
                chunk, first : first + z.window, :
            ]
        slots[k, z.wide :, :] = jnp.where(k > at.position, ahead, behind)
    store = pltpu.make_async_copy(slots, slots_far, sem.at[7])
    store.start()
    loads[5].wait()
    loads[6].wait()
    store.wait()


def static_kernel(z, live, operator, inverse, margin_in, vectors_t, *refs):
    stack, first, second, margin, sem = refs
    side, modes, picked = z.side, z.modes, z.picked
    load = pltpu.make_async_copy(margin_in, margin, sem)
    load.start()
    load.wait()
    at = Place(z, live, margin)
    rows = jnp.concatenate([at.ahead(operator), at.behind(operator)], axis=0)
    kept = at.kept_columns()
    stack[:modes, :] = vectors_t[...]
    masked = (vectors_t[...].astype(F32) * kept).astype(BF16)
    picks = at.lent_columns()
    columns = mm(rows, picks).astype(BF16)
    up = nt(masked, rows).astype(BF16)
    first[...] = jnp.concatenate(
        [columns[:side, :side], columns[:side, side:], up[:, :side]], axis=0
    )
    second[...] = jnp.concatenate(
        [columns[side:, side:], columns[side:, :side], up[:, side:]], axis=0
    )
    stack[modes : modes + picked, :] = jnp.concatenate(
        [at.ahead(inverse), at.behind(inverse)], axis=0
    )
    value = (rows.astype(F32) * kept[:1]).astype(BF16)
    stack[modes + picked :, :] = mm(value, inverse[...]).astype(BF16)


def send(z, at, stack, low, momentum, copies, every_out, sem, first, second, far):
    side, modes = z.side, z.modes
    mine = mm(stack[:modes, :], low).astype(BF16)

    def put(k, carry):
        copies[k] = mine
        return carry

    lax.fori_loop(0, z.subs * z.groups, put, 0, unroll=min(32, z.subs * z.groups))
    copy = pltpu.make_async_copy(copies, every_out, sem)
    copy.start()
    value = mm(stack[modes:, :], low)
    pieces = [value[k * side : (k + 1) * side] for k in range(4)]
    if momentum is not None:
        pieces[2] = pieces[2] + momentum[0]
        pieces[3] = pieces[3] + momentum[1]
    pieces = [piece.astype(BF16) for piece in pieces]
    first[:side, :], second[:side, :] = pieces[0], pieces[1]
    first[side:, :], second[side:, :] = pieces[2], pieces[3]
    if z.folded:
        far[0][...] = jnp.where(at.has_right2, pieces[0], pieces[1])
    else:
        far[0][...], far[1][...] = pieces[0], pieces[1]
    return copy


def second_kernel(z, live, slots, source, stack, resid, every_out, first, second, *rest):
    far, (copies, sem) = rest[:-2], rest[-2:]
    at = Place(z, live)
    left = slots[jnp.maximum(at.position - 1, 0), z.wide + z.modes :, :]
    right = slots[jnp.minimum(at.position + 1, z.subs - 1), z.wide + z.modes :, :]
    value = jnp.concatenate(
        [
            jnp.where(at.row_mask(), source[...], 0.0),
            jnp.where(at.has_left, left.astype(F32), 0.0),
            jnp.where(at.has_right, right.astype(F32), 0.0),
        ],
        axis=0,
    )
    resid[...] = value
    low = value.astype(BF16)
    send(z, at, stack, low, None, copies, every_out, sem, first, second, far).wait()


def window_kernel(z, turn, live, resid, inverse_far, operator_far, *refs):
    if turn:
        part_in, coarse, stack, *refs = refs
        if turn > 1:
            solution_far, *refs = refs
        part, product, solution_out, *refs = refs
        inverse, operator, direction, solution, sem = refs
        more = [(solution_far, solution)] if turn > 1 else []
    else:
        slots, lent, stack, margin_in, left_static, right_static, *refs = refs
        part, product, spread, panels, columns, inverse, operator, margin, sem = refs
        more = [(margin_in, margin)]
    loads = start_all(sem, (inverse_far, inverse), (operator_far, operator), *more)
    at = Place(z, live)
    if turn:
        index = at.position - z.base(at.position)
        own = coarse[pl.ds(pl.multiple_of(index * z.modes, z.modes), z.modes), :]
        direction[...] = part_in[...] + at.kept(tn(stack[: z.modes, :], own))
        step = STEP_SIZES[turn - 1] * direction[: z.owned, :]
        if turn > 1:
            loads[2].wait()
            step = solution[...] + step
        solution[...] = step
        store = pltpu.make_async_copy(solution, solution_out, sem.at[3])
        store.start()
    else:
        for k in range(z.subs):
            for chunk in range(z.chunks):
                start = (k * z.chunks + chunk) * z.loads
                panels[:, start : start + z.loads] = slots[
                    k, chunk * z.window : (chunk + 1) * z.window, :
                ]
        loads[2].wait()
        picks = Place(z, live, margin).lent_columns()
        loads[1].wait()
        columns[...] = mm(operator[...], picks).astype(BF16)
        masked = (stack[: z.modes, :].astype(F32) * at.kept_columns()).astype(BF16)
        lifted = nt(masked, operator[...]).astype(BF16)
        spread_corrections(z, at, slots, lent, lifted, left_static, right_static, spread)
    loads[0].wait()
    value = at.kept(mm(inverse[...], resid[...].astype(BF16)))
    if turn:
        value = value + MOMENTUM[turn] * direction[...]
    part[...] = value
    if turn:
        loads[1].wait()
    product[...] = mm(operator[...], value.astype(BF16))
    if turn:
        store.wait()


def spread_corrections(z, at, slots, lent, lifted, left_static, right_static, spread):
    side, modes = z.side, z.modes
    row = lax.broadcasted_iota(jnp.int32, (modes, 2 * z.window), 0)
    col = lax.broadcasted_iota(jnp.int32, (modes, 2 * z.window), 1)
    base = z.base(at.position)

    def theirs(offset):
        index = jnp.clip(at.position + offset, 0, z.subs - 1)
        return slots[index, z.wide : z.wide + modes, :]

    left, right = left_static[2 * side :, :], right_static[2 * side :, :]
    halves = (
        [
            (theirs(-1), -1, at.has_left),
            (theirs(1), 1, at.has_right),
            (theirs(-2), -2, at.has_left2),
            (theirs(2), 2, at.has_right2),
            (lent[:modes, :], 0, True),
            (lent[modes:, :], 0, True),
        ],
        [(left, -1, at.has_left), (right, 1, at.has_right)]
        + [(lifted[:, k : k + side], 0, True) for k in range(0, z.order, side)],
    )
    for segment in range(z.segments):
        total = jnp.zeros((side, 2 * z.window), F32)
        for half, entries in enumerate(halves):
            if segment < len(entries):
                transposed, offset, have = entries[segment]
                first = half * z.window + (at.position + offset - base) * modes
                place = jnp.where(have, 1.0, 0.0) * jnp.where(col == first + row, 1.0, 0.0)
                total = total + tn(transposed, place.astype(BF16))
        spread[segment * side : (segment + 1) * side, :] = total.astype(BF16)


def main_kernel(z, turn, live, margin_in, *refs):
    last = turn == ITERS - 1
    every, panels, spread, columns, product, resid_in, *refs = refs
    ahead_in, behind_in, left_got, right_got, *refs = refs
    far_left, far_right, left_static, right_static, *refs = refs
    if last:
        part, stack, solution_far, solution_out, resid_out, *refs = refs
        margin, error, resid, direction, solution, sem = refs
        loads = start_all(sem, (margin_in, margin), (solution_far, solution))
    else:
        part, stack, resid, every_out, first, second, *refs = refs
        far, (coarse_out, part_out, margin, error, copies, sem) = refs[:-6], refs[-6:]
        loads = start_all(sem, (margin_in, margin))
    at = Place(z, live)
    side, owned, modes = z.side, z.owned, z.modes

    coarse = jnp.zeros((z.window, z.loads), F32)
    for start in range(0, panels.shape[1], 4 * z.loads):
        stop = min(start + 4 * z.loads, panels.shape[1])
        coarse = coarse + mm(panels[:, start:stop], every[start:stop, :])
    coarse = coarse.astype(BF16)
    nothing = jnp.zeros_like(coarse)
    twice = jnp.concatenate(
        [jnp.concatenate([coarse, nothing], axis=1), jnp.concatenate([nothing, coarse], axis=1)],
        axis=0,
    )
    taken = mm(spread[...], twice)

    def term(segment):
        return taken[segment * side : (segment + 1) * side, : z.loads]

    def other_term(start, rows):
        return taken[start : start + rows, z.loads :]


    def masked(have, value):
        return jnp.where(have, value.astype(F32), 0.0)

    from_left = masked(at.has_left, left_got[:side, :]) + term(0)
    from_right = masked(at.has_right, right_got[:side, :]) + term(1)
    halo = jnp.concatenate([from_left, from_right], axis=0)
    from_left2 = masked(at.has_left2, far_left[...]) + term(2)
    from_right2 = masked(at.has_right2, far_right[...]) + term(3)
    loads[0].wait()
    at.lend(margin[0, 0], margin[0, 1])
    to_right = (ahead_in[:side, :].astype(F32) + term(4)).astype(BF16)
    to_left = (behind_in[:side, :].astype(F32) + term(5)).astype(BF16)
    if last:
        index = at.position - z.base(at.position)
        error[: z.window, :] = coarse.astype(F32)
        own = error[pl.ds(pl.multiple_of(index * modes, modes), modes), :].astype(BF16)
        direction[...] = part[...] + at.kept(tn(stack[:modes, :], own))
        at.add_lent(direction, 1.0, from_left, from_right)
        loads[1].wait()
        solution[...] = solution[...] + STEP_SIZES[turn] * direction[:owned, :]
        store_solution = pltpu.make_async_copy(solution, solution_out, sem.at[2])
        store_solution.start()

    def borrowed(have, got, statics, far, near, start):
        rows = jnp.concatenate([statics[:side, :], statics[side : 2 * side, :]], axis=1)
        value = mm(rows, jnp.concatenate([far.astype(BF16), near], axis=0))
        return masked(have, value + got[side:, :].astype(F32)) + other_term(start, side)

    applied = product[...] + other_term(2 * side, z.order) + mm(columns[...], halo.astype(BF16))
    left = borrowed(at.has_left, left_got, left_static, from_left2, to_left, 0)
    right = borrowed(at.has_right, right_got, right_static, from_right2, to_right, side)
    error[...] = applied
    resid[...] = resid_in[...] - STEP_SIZES[turn] * at.kept(applied)
    at.add_lent(resid, -STEP_SIZES[turn], left, right)
    if last:
        store = pltpu.make_async_copy(resid.at[pl.ds(0, owned), :], resid_out, sem.at[3])
        store.start()
        store.wait()
        store_solution.wait()
    else:
        low = resid[...].astype(BF16)
        beta = MOMENTUM[turn + 1]
        momentum = beta * at.ahead(error), beta * at.behind(error)
        store = send(z, at, stack, low, momentum, copies, every_out, sem.at[2], first, second, far)
        coarse_out[...] = coarse
        at.add_lent(part_out, 1.0, from_left, from_right, part)
        store.wait()


def body(
    right_side, live_rows, margin_blocks, local_operator, local_inverse, deflation, coarse_inverse
):
    z = Sizes(right_side, deflation, coarse_inverse)
    source = right_side[0, 0]
    operator = Far(local_operator[0, 0])
    inverse = Far(local_inverse[0, 0])
    vectors_t = deflation[0, 0].T
    margin = Far(margin_blocks.reshape(1, -1))
    scalars = (live_rows,)
    owned, order, loads, modes, side = z.owned, z.order, z.loads, z.modes, z.side
    devices = z.subs * z.groups

    pick = pltpu.SMEM((1, margin_blocks.shape[-1]), jnp.int32)
    sems = pltpu.SemaphoreType.DMA
    square = pltpu.VMEM((order, order), BF16)

    def part(function, *more):
        return functools.partial(function, z, *more)

    def low(*dims):
        return shape(*dims, dtype=BF16)

    def exchange(first, second):
        return lax.ppermute(first, "sub", ring(1)), lax.ppermute(second, "sub", ring(-1))

    def ring(offset):
        return [(i, (i + offset) % z.subs) for i in range(z.subs)]

    panel = coarse_inverse.reshape(-1, z.chunks, loads).swapaxes(0, 1)
    slots, lent, spot, operator_near, inverse_near = run(
        part(first_kernel),
        [
            Far(low(z.subs, z.wide + modes + z.blk, loads)),
            low(2 * modes, side),
            shape(1, margin_blocks.shape[-1], dtype=jnp.int32),
            low(order, order),
            low(order, order),
        ],
        [Far(source), Far(vectors_t), Far(panel), margin, operator, inverse],
        (),
        [
            pltpu.VMEM((z.subs, z.wide + modes + z.blk, loads), BF16),
            pltpu.VMEM(source.shape, F32),
            pltpu.VMEM(vectors_t.shape, BF16),
            pltpu.VMEM(panel.shape, BF16),
            pick,
            sems((8,)),
        ],
    )
    slots = lax.all_to_all(slots, "sub", 0, 0, tiled=True)
    stack, first, second = run(
        part(static_kernel),
        [low(z.stack, order)]
        + [low(2 * side + modes, loads)] * 2,
        [operator_near, inverse_near, spot, vectors_t],
        scalars,
        [pick, sems(())],
    )
    left_static, right_static = exchange(first, second)
    sent = [shape(order, loads), Far(low(devices, modes, loads))]
    sent += [low(2 * side, loads)] * 2 + [low(side, loads)] * (1 if z.folded else 2)
    copies = pltpu.VMEM((devices, modes, loads), BF16)
    resid, every, first, second, *far = run(
        part(second_kernel), sent, [slots, source, stack], scalars, [copies, sems(())]
    )
    full = shape(order, loads)
    floor = pltpu.VMEM((order, loads), F32)
    solution = None
    for turn in range(ITERS):
        last = turn == ITERS - 1
        every = lax.all_to_all(every, ("sub", "grp"), 0, 0, tiled=True)
        every = every.reshape(devices * modes, loads)
        left_got, right_got = exchange(first, second)
        if z.folded:
            far_left = far_right = lax.ppermute(far[0], "sub", ring(2))
        else:
            far_left = lax.ppermute(far[0], "sub", ring(2))
            far_right = lax.ppermute(far[1], "sub", ring(-2))
        args = [resid, inverse, operator]
        if turn:
            args += [error, coarse, stack]
            args += [solution] if turn > 1 else []
            outs = [full, full, Far(shape(owned, loads))]
            work = [square, square, floor, pltpu.VMEM((owned, loads), F32), sems((4,))]
        else:
            args += [slots, lent, stack, spot, left_static, right_static]
            outs = [full, full, low(z.segments * side, 2 * z.window)]
            outs += [low(z.window, z.subs * z.chunks * loads), low(order, 2 * side)]
            work = [square, square, pick, sems((3,))]
        error, product, *more = run(
            part(window_kernel, turn),
            outs,
            args,
            scalars,
            work,
            aliases={len(scalars) + 3: 0} if turn else None,
        )
        if turn:
            solution = Far(more[0])
        else:
            spread, panels, columns = more
        args = [spot, every, panels, spread, columns, product, resid]
        args += [first, second, left_got, right_got, far_left, far_right]
        args += [left_static, right_static]
        if last:
            solution, resid = run(
                part(main_kernel, turn),
                [Far(shape(owned, loads))] * 2,
                args + [error, stack, solution],
                scalars,
                [pick, floor, floor, floor, pltpu.VMEM((owned, loads), F32), sems((4,))],
            )
        else:
            outs = sent + [low(z.window, loads), full]
            resid, every, first, second, *far, coarse, error = run(
                part(main_kernel, turn),
                outs,
                args + [error, stack],
                scalars,
                [pick, floor, copies, sems((3,))],
                aliases={len(scalars) + len(args): len(outs) - 1},
            )
    return (solution[None, None], resid[None, None])


def solution(mesh):
    return jax.shard_map(
        body,
        mesh=mesh,
        in_specs=(
            P("grp", "sub", None, None),
            P("grp", "sub"),
            P("grp", "sub", None),
            P("grp", "sub", None, None),
            P("grp", "sub", None, None),
            P("grp", "sub", None, None),
            P("grp", "sub"),
        ),
        out_specs=(P("grp", "sub", None, None), P("grp", "sub", None, None)),
        check_vma=False,
    )
```

```python
import functools

import jax
import jax.numpy as jnp
from jax import lax
from jax.experimental import pallas as pl
from jax.experimental.pallas import tpu as pltpu
from jax.sharding import PartitionSpec as P

ITERS = 3


STEP_SIZES = (0.8, 0.9, 1.0)
MOMENTUM = (0.0, 0.3, 0.3)

F32 = jnp.float32
BF16 = jnp.bfloat16


def mm(a, b):
    return jnp.dot(a, b, preferred_element_type=F32)


def tn(a, b):
    return lax.dot_general(a, b, (((0,), (0,)), ((), ())), preferred_element_type=F32)


def nt(a, b):
    return lax.dot_general(a, b, (((1,), (1,)), ((), ())), preferred_element_type=F32)


def run(kernel, outs, args, scalars=(), scratch=(), flops=1 << 22, aliases=None):
    nbytes = sum(x.size * x.dtype.itemsize for x in map(bare, [*args, *outs]))
    return pl.pallas_call(
        kernel,
        out_shape=[held(x) for x in outs],
        in_specs=[pl.BlockSpec(memory_space=pltpu.SMEM)] * len(scalars) + [spec(x) for x in args],
        out_specs=[spec(x) for x in outs],
        scratch_shapes=list(scratch),
        input_output_aliases=aliases or {},
        compiler_params=pltpu.CompilerParams(vmem_limit_bytes=24 << 20),
        cost_estimate=pl.CostEstimate(flops=flops, bytes_accessed=nbytes, transcendentals=0),
    )(
        *scalars,
        *map(given, args),
    )


class Far:
    def __init__(self, array):
        self.array = array


def bare(x):
    return x.array if isinstance(x, Far) else x


def held(x):
    return pltpu.HBM(x.array.shape, x.array.dtype) if isinstance(x, Far) else x


def given(x):
    return pltpu.with_memory_space_constraint(x.array, pltpu.HBM) if isinstance(x, Far) else x


def spec(x):
    return pl.BlockSpec(memory_space=pltpu.HBM if isinstance(x, Far) else pltpu.VMEM)


def shape(*dims, dtype=F32):
    return jax.ShapeDtypeStruct(dims, dtype)


class Sizes:
    def __init__(self, right_side, deflation, coarse_inverse):
        self.owned, self.loads = right_side.shape[-2:]
        self.order, self.modes = deflation.shape[-2:]
        self.blk = (self.order - self.owned) // 2
        self.side = 2 * self.blk
        self.subs = lax.axis_size("sub")
        self.groups = lax.axis_size("grp")
        self.near = min(self.subs, 5)
        self.chunks = coarse_inverse.shape[1] // self.loads
        self.window = self.near * self.modes
        self.wide = self.window * self.chunks
        self.picked = 2 * self.side
        self.stack = self.modes + 2 * self.picked
        self.folded = self.subs == 4
        self.lead = self.modes + self.blk
        self.opening = 2 if self.folded else 1
        self.segments = max(6, 2 + self.order // self.side)

    def base(self, position):
        return jnp.clip(position - 2, 0, self.subs - self.near)


class Place:
    def __init__(self, z, live, margin=None):
        self.z = z
        self.position = lax.axis_index("sub")
        self.live = None if live is None else live[0, 0]
        self.has_left = self.position > 0
        self.has_right = self.position < z.subs - 1
        self.has_left2 = self.position > 1
        self.has_right2 = self.position < z.subs - 2
        if margin is not None:
            self.lend(margin[0, 0], margin[0, 1])

    def lend(self, right, left):
        blk = self.z.blk
        self.give_right = pl.multiple_of(right * blk, blk)
        self.give_left = pl.multiple_of(left * blk, blk)

    def row_mask(self):
        z = self.z
        rows = lax.broadcasted_iota(jnp.int32, (z.owned, z.loads), 0)
        return rows < self.live

    def kept(self, value):
        z = self.z
        low = value[z.owned : z.owned + z.blk]
        high = value[z.owned + z.blk :]
        return jnp.concatenate(
            [
                jnp.where(self.row_mask(), value[: z.owned], 0.0),
                jnp.where(self.has_left, low, 0.0),
                jnp.where(self.has_right, high, 0.0),
            ],
            axis=0,
        )

    def kept_columns(self):
        z = self.z
        col = lax.broadcasted_iota(jnp.int32, (z.modes, z.order), 1)
        limit = jnp.where(self.has_left, z.owned + z.blk, z.owned)
        kept = (col < self.live) | ((col >= z.owned) & (col < limit))
        return jnp.where(kept | ((col >= z.owned + z.blk) & self.has_right), 1.0, 0.0)

    def lent_columns(self):
        z = self.z
        return jnp.concatenate(
            [
                selection(z, self.give_left, z.owned),
                selection(z, self.give_right, z.owned + z.blk),
            ],
            axis=1,
        )

    def right_block(self, ref):
        return ref[pl.ds(self.give_right, self.z.blk), :]

    def left_block(self, ref):
        return ref[pl.ds(self.give_left, self.z.blk), :]

    def ahead(self, ref):
        z = self.z
        return jnp.concatenate([ref[z.owned + z.blk :, :], self.right_block(ref)], axis=0)

    def behind(self, ref):
        z = self.z
        return jnp.concatenate([ref[z.owned : z.owned + z.blk, :], self.left_block(ref)], axis=0)

    def add_lent(self, target, scale, from_left, from_right, source=None, rims=True):
        z = self.z
        source = target if source is None else source
        pieces = [
            (pl.ds(self.give_left, z.blk), from_left[: z.blk]),
            (pl.ds(self.give_right, z.blk), from_right[: z.blk]),
        ]
        if rims:
            pieces += [
                (slice(z.owned, z.owned + z.blk), from_left[z.blk :]),
                (slice(z.owned + z.blk, z.order), from_right[z.blk :]),
            ]
        for spot, value in pieces:
            target[spot, :] = source[spot, :] + (value if scale == 1.0 else scale * value)


def selection(z, first, second):
    row = lax.broadcasted_iota(jnp.int32, (z.order, z.side), 0)
    col = lax.broadcasted_iota(jnp.int32, (z.order, z.side), 1)
    return (row == jnp.where(col < z.blk, first + col, second - z.blk + col)).astype(BF16)


def start_all(sem, *pairs):
    copies = [
        pltpu.make_async_copy(source, target, sem.at[k])
        for k, (source, target) in enumerate(pairs)
    ]
    for copy in copies:
        copy.start()
    return copies


def first_kernel(
    z, source_far, vectors_far, panel_far, margin_far, operator_far, inverse_far, *refs
):
    if z.folded:
        ahead_out, behind_out, lent, spot, operator, inverse, *scratch = refs
    else:
        slots_far, lent, spot, operator, inverse, slots, *scratch = refs
    source, vectors_t, panel, margin, sem = scratch
    loads = start_all(
        sem,
        (margin_far, margin),
        (vectors_far, vectors_t),
        (panel_far, panel),
        (source_far, source),
        (margin_far, spot),
        (operator_far, operator),
        (inverse_far, inverse),
    )
    loads[0].wait()
    at = Place(z, None, margin)
    loads[1].wait()
    rows = selection(z, z.owned + z.blk, at.give_right)
    ahead_vectors = mm(vectors_t[...], rows).astype(BF16)
    rows = selection(z, z.owned, at.give_left)
    behind_vectors = mm(vectors_t[...], rows).astype(BF16)
    lent[...] = jnp.concatenate([ahead_vectors, behind_vectors], axis=0)
    loads[2].wait()
    loads[4].wait()
    loads[3].wait()
    ahead = jnp.concatenate([ahead_vectors, at.right_block(source).astype(BF16)], axis=0)
    behind = jnp.concatenate([behind_vectors, at.left_block(source).astype(BF16)], axis=0)
    if z.folded:
        for out, value in ((ahead_out, ahead), (behind_out, behind)):
            out[: z.lead, :] = value
            put_panel(z, out, z.lead, panel)
    else:
        for k in range(z.subs):
            first = min(max(k - 2, 0), z.subs - z.near) * z.modes
            for chunk in range(z.chunks):
                slots[k, chunk * z.window : (chunk + 1) * z.window, :] = panel[
                    chunk, first : first + z.window, :
                ]
            slots[k, z.wide :, :] = jnp.where(k > at.position, ahead, behind)
        store = pltpu.make_async_copy(slots, slots_far, sem.at[7])
        store.start()
    loads[5].wait()
    loads[6].wait()
    if not z.folded:
        store.wait()


def put_panel(z, out, start, panel):
    for chunk in range(z.chunks):
        first = start + chunk * z.window
        out[first : first + z.window, :] = panel[chunk, :, :]


def static_kernel(z, live, operator, inverse, margin_in, vectors_t, *refs):
    stack, first, second, margin, sem = refs
    side, modes, picked = z.side, z.modes, z.picked
    load = pltpu.make_async_copy(margin_in, margin, sem)
    load.start()
    load.wait()
    at = Place(z, live, margin)
    rows = jnp.concatenate([at.ahead(operator), at.behind(operator)], axis=0)
    kept = at.kept_columns()
    stack[:modes, :] = vectors_t[...]
    masked = (vectors_t[...].astype(F32) * kept).astype(BF16)
    picks = at.lent_columns()
    columns = mm(rows, picks).astype(BF16)
    up = nt(masked, rows).astype(BF16)
    first[...] = jnp.concatenate(
        [columns[:side, :side], columns[:side, side:], up[:, :side]], axis=0
    )
    second[...] = jnp.concatenate(
        [columns[side:, side:], columns[side:, :side], up[:, side:]], axis=0
    )
    stack[modes : modes + picked, :] = jnp.concatenate(
        [at.ahead(inverse), at.behind(inverse)], axis=0
    )
    value = (rows.astype(F32) * kept[:1]).astype(BF16)
    stack[modes + picked :, :] = mm(value, inverse[...]).astype(BF16)


def send(z, at, stack, low, momentum, copies, every_out, sem, first, second, far):
    side, modes = z.side, z.modes
    mine = mm(stack[:modes, :], low).astype(BF16)

    def put(k, carry):
        copies[k] = mine
        return carry

    lax.fori_loop(0, z.subs * z.groups, put, 0, unroll=min(32, z.subs * z.groups))
    copy = pltpu.make_async_copy(copies, every_out, sem)
    copy.start()
    value = mm(stack[modes:, :], low)
    pieces = [value[k * side : (k + 1) * side] for k in range(4)]
    if momentum is not None:
        pieces[2] = pieces[2] + momentum[0]
        pieces[3] = pieces[3] + momentum[1]
    pieces = [piece.astype(BF16) for piece in pieces]
    first[:side, :], second[:side, :] = pieces[0], pieces[1]
    first[side:, :], second[side:, :] = pieces[2], pieces[3]
    if z.folded:
        far[0][:side, :] = jnp.where(at.has_right2, pieces[0], pieces[1])
    else:
        far[0][...], far[1][...] = pieces[0], pieces[1]
    return copy


def second_kernel(z, live, source, stack, *refs):
    at = Place(z, live)
    if z.folded:
        left_open, right_open, lent, panel, *refs = refs
        left, right = left_open[z.modes : z.lead, :], right_open[z.modes : z.lead, :]
    else:
        slots, *refs = refs
        left = slots[jnp.maximum(at.position - 1, 0), z.wide + z.modes :, :]
        right = slots[jnp.minimum(at.position + 1, z.subs - 1), z.wide + z.modes :, :]
    resid, every_out, first, second, *rest = refs
    far, (copies, sem) = rest[:-2], rest[-2:]
    value = jnp.concatenate(
        [
            jnp.where(at.row_mask(), source[...], 0.0),
            jnp.where(at.has_left, left.astype(F32), 0.0),
            jnp.where(at.has_right, right.astype(F32), 0.0),
        ],
        axis=0,
    )
    resid[...] = value
    low = value.astype(BF16)
    store = send(z, at, stack, low, None, copies, every_out, sem, first, second, far)
    if z.folded:
        mine = jnp.where(at.has_right2, lent[: z.modes, :], lent[z.modes :, :])
        far[0][z.side : z.side + z.modes, :] = mine
        put_panel(z, far[0], z.side + z.modes, panel)
    store.wait()


def window_kernel(z, turn, live, resid, inverse_far, operator_far, *refs):
    if turn:
        part_in, coarse, stack, *refs = refs
        if turn > 1:
            solution_far, *refs = refs
        part, product, solution_out, *refs = refs
        inverse, operator, direction, solution, sem = refs
        more = [(solution_far, solution)] if turn > 1 else []
    else:
        opening, refs = refs[: z.opening], refs[z.opening :]
        lent, stack, margin_in, left_static, right_static, *refs = refs
        part, product, spread, columns, *refs = refs
        panels, (inverse, operator, margin, sem) = refs[:-4], refs[-4:]
        more = [(margin_in, margin)]
    loads = start_all(sem, (inverse_far, inverse), (operator_far, operator), *more)
    at = Place(z, live)
    if turn:
        index = at.position - z.base(at.position)
        own = coarse[pl.ds(pl.multiple_of(index * z.modes, z.modes), z.modes), :]
        direction[...] = part_in[...] + at.kept(tn(stack[: z.modes, :], own))
        step = STEP_SIZES[turn - 1] * direction[: z.owned, :]
        if turn > 1:
            loads[2].wait()
            step = solution[...] + step
        solution[...] = step
        store = pltpu.make_async_copy(solution, solution_out, sem.at[3])
        store.start()
    else:
        if not z.folded:
            for k in range(z.subs):
                for chunk in range(z.chunks):
                    start = (k * z.chunks + chunk) * z.loads
                    panels[0][:, start : start + z.loads] = opening[0][
                        k, chunk * z.window : (chunk + 1) * z.window, :
                    ]
        loads[2].wait()
        picks = Place(z, live, margin).lent_columns()
        loads[1].wait()
        columns[...] = mm(operator[...], picks).astype(BF16)
        masked = (stack[: z.modes, :].astype(F32) * at.kept_columns()).astype(BF16)
        lifted = nt(masked, operator[...]).astype(BF16)
        spread_corrections(z, at, opening, lent, lifted, left_static, right_static, spread)
    loads[0].wait()
    value = at.kept(mm(inverse[...], resid[...].astype(BF16)))
    if turn:
        value = value + MOMENTUM[turn] * direction[...]
    part[...] = value
    if turn:
        loads[1].wait()
    product[...] = mm(operator[...], value.astype(BF16))
    if turn:
        store.wait()


def spread_corrections(z, at, opening, lent, lifted, left_static, right_static, spread):
    side, modes = z.side, z.modes
    row = lax.broadcasted_iota(jnp.int32, (modes, 2 * z.window), 0)
    col = lax.broadcasted_iota(jnp.int32, (modes, 2 * z.window), 1)
    base = z.base(at.position)

    def theirs(offset):
        if z.folded:
            return opening[0 if offset < 0 else 1][:modes, :]
        index = jnp.clip(at.position + offset, 0, z.subs - 1)
        return opening[0][index, z.wide : z.wide + modes, :]

    left, right = left_static[2 * side :, :], right_static[2 * side :, :]
    halves = (
        [
            (theirs(-1), -1, at.has_left),
            (theirs(1), 1, at.has_right),
            None if z.folded else (theirs(-2), -2, at.has_left2),
            None if z.folded else (theirs(2), 2, at.has_right2),
            (lent[:modes, :], 0, True),
            (lent[modes:, :], 0, True),
        ],
        [(left, -1, at.has_left), (right, 1, at.has_right)]
        + [(lifted[:, k : k + side], 0, True) for k in range(0, z.order, side)],
    )
    for segment in range(z.segments):
        total = jnp.zeros((side, 2 * z.window), F32)
        for half, entries in enumerate(halves):
            if segment < len(entries) and entries[segment] is not None:
                transposed, offset, have = entries[segment]
                first = half * z.window + (at.position + offset - base) * modes
                place = jnp.where(have, 1.0, 0.0) * jnp.where(col == first + row, 1.0, 0.0)
                total = total + tn(transposed, place.astype(BF16))
        spread[segment * side : (segment + 1) * side, :] = total.astype(BF16)


def main_kernel(z, turn, live, margin_in, *refs):
    last = turn == ITERS - 1
    gather = z.folded and not turn
    if gather:
        every, left_open, right_open, panel, spread, columns, product, resid_in, *refs = refs
    else:
        every, panels, spread, columns, product, resid_in, *refs = refs
    ahead_in, behind_in, left_got, right_got, *refs = refs
    far_left, far_right, left_static, right_static, *refs = refs
    if z.folded:
        far_static, *refs = refs
    if last:
        part, stack, solution_far, solution_out, resid_out, *refs = refs
        margin, error, resid, direction, solution, sem = refs
        loads = start_all(sem, (margin_in, margin), (solution_far, solution))
    else:
        part, stack, resid, every_out, first, second, *refs = refs
        far, (coarse_out, part_out, margin, error, copies, sem) = refs[:-6], refs[-6:]
        if gather:
            far, panels = far[:-1], far[-1]
        loads = start_all(sem, (margin_in, margin))
    at = Place(z, live)
    side, owned, modes = z.side, z.owned, z.modes

    if gather:
        start = z.side + modes
        pieces = (
            panel[...].reshape(z.wide, z.loads),
            right_open[z.lead :, :],
            far_left[start:, :],
            left_open[z.lead :, :],
        )
        for k in range(z.subs):
            turns = (k + z.subs - at.position) % z.subs
            piece = pieces[0]
            for index in range(1, z.subs):
                piece = jnp.where(turns == index, pieces[index], piece)
            for chunk in range(z.chunks):
                start = (k * z.chunks + chunk) * z.loads
                panels[:, start : start + z.loads] = piece[
                    chunk * z.window : (chunk + 1) * z.window, :
                ]
    coarse = jnp.zeros((z.window, z.loads), F32)
    for start in range(0, panels.shape[1], 4 * z.loads):
        stop = min(start + 4 * z.loads, panels.shape[1])
        coarse = coarse + mm(panels[:, start:stop], every[start:stop, :])
    coarse = coarse.astype(BF16)
    nothing = jnp.zeros_like(coarse)
    twice = jnp.concatenate(
        [jnp.concatenate([coarse, nothing], axis=1), jnp.concatenate([nothing, coarse], axis=1)],
        axis=0,
    )
    rows = owned if last else z.order
    taken = mm(spread[: max(6 * side, 2 * side + rows), :], twice)

    def term(segment):
        return taken[segment * side : (segment + 1) * side, : z.loads]

    def other_term(start, count):
        return taken[start : start + count, z.loads :]

    def masked(have, value):
        return jnp.where(have, value.astype(F32), 0.0)

    from_left = masked(at.has_left, left_got[:side, :]) + term(0)
    from_right = masked(at.has_right, right_got[:side, :]) + term(1)
    halo = jnp.concatenate([from_left, from_right], axis=0)

    def correction(offset):
        index = jnp.clip(at.position + offset - z.base(at.position), 0, z.near - 1)
        error[: z.window, :] = coarse.astype(F32)
        return error[pl.ds(pl.multiple_of(index * modes, modes), modes), :].astype(BF16)

    if z.folded:
        there = correction(jnp.where(at.has_left2, -2, 2))
        from_far = far_left[:side, :].astype(F32) + tn(far_static[side : side + modes, :], there)
        from_left2, from_right2 = masked(at.has_left2, from_far), masked(at.has_right2, from_far)
    else:
        from_left2 = masked(at.has_left2, far_left[...]) + term(2)
        from_right2 = masked(at.has_right2, far_right[...]) + term(3)
    loads[0].wait()
    at.lend(margin[0, 0], margin[0, 1])
    to_right = (ahead_in[:side, :].astype(F32) + term(4)).astype(BF16)
    to_left = (behind_in[:side, :].astype(F32) + term(5)).astype(BF16)
    if last:
        lifted = tn(stack[:modes, :owned], correction(0))
        lifted = jnp.where(at.row_mask(), lifted, 0.0)
        direction[...] = part[:owned, :] + lifted
        at.add_lent(direction, 1.0, from_left, from_right, rims=False)
        loads[1].wait()
        solution[...] = solution[...] + STEP_SIZES[turn] * direction[...]
        store_solution = pltpu.make_async_copy(solution, solution_out, sem.at[2])
        store_solution.start()

    count = z.blk if last else side

    def borrowed(have, got, statics, far, near, start):
        both = jnp.concatenate([statics[:count, :], statics[side : side + count, :]], axis=1)
        value = mm(both, jnp.concatenate([far.astype(BF16), near], axis=0))
        value = masked(have, value + got[side : side + count, :].astype(F32))
        return value + other_term(start, count)

    applied = product[:rows, :] + other_term(2 * side, rows)
    applied = applied + mm(columns[:rows, :], halo.astype(BF16))
    left = borrowed(at.has_left, left_got, left_static, from_left2, to_left, 0)
    right = borrowed(at.has_right, right_got, right_static, from_right2, to_right, side)
    if last:
        applied = jnp.where(at.row_mask(), applied, 0.0)
        resid[...] = resid_in[:owned, :] - STEP_SIZES[turn] * applied
    else:
        error[...] = applied
        resid[...] = resid_in[...] - STEP_SIZES[turn] * at.kept(applied)
    at.add_lent(resid, -STEP_SIZES[turn], left, right, rims=not last)
    if last:
        store = pltpu.make_async_copy(resid, resid_out, sem.at[3])
        store.start()
        store.wait()
        store_solution.wait()
    else:
        low = resid[...].astype(BF16)
        beta = MOMENTUM[turn + 1]
        momentum = beta * at.ahead(error), beta * at.behind(error)
        store = send(z, at, stack, low, momentum, copies, every_out, sem.at[2], first, second, far)
        coarse_out[...] = coarse
        at.add_lent(part_out, 1.0, from_left, from_right, part)
        store.wait()


def body(
    right_side, live_rows, margin_blocks, local_operator, local_inverse, deflation, coarse_inverse
):
    z = Sizes(right_side, deflation, coarse_inverse)
    source = right_side[0, 0]
    operator = Far(local_operator[0, 0])
    inverse = Far(local_inverse[0, 0])
    vectors_t = deflation[0, 0].T
    margin = Far(margin_blocks.reshape(1, -1))
    scalars = (live_rows,)
    owned, order, loads, modes, side = z.owned, z.order, z.loads, z.modes, z.side
    devices = z.subs * z.groups

    pick = pltpu.SMEM((1, margin_blocks.shape[-1]), jnp.int32)
    sems = pltpu.SemaphoreType.DMA
    square = pltpu.VMEM((order, order), BF16)

    def part(function, *more):
        return functools.partial(function, z, *more)

    def low(*dims):
        return shape(*dims, dtype=BF16)

    def exchange(first, second):
        return lax.ppermute(first, "sub", ring(1)), lax.ppermute(second, "sub", ring(-1))

    def ring(offset):
        return [(i, (i + offset) % z.subs) for i in range(z.subs)]

    panel = coarse_inverse.reshape(-1, z.chunks, loads).swapaxes(0, 1)
    lead = z.lead + z.wide
    *opening, lent, spot, operator_near, inverse_near = run(
        part(first_kernel),
        ([low(lead, loads)] * 2 if z.folded else [Far(low(z.subs, lead, loads))])
        + [
            low(2 * modes, side),
            shape(1, margin_blocks.shape[-1], dtype=jnp.int32),
            low(order, order),
            low(order, order),
        ],
        [Far(source), Far(vectors_t), Far(panel), margin, operator, inverse],
        (),
        ([] if z.folded else [pltpu.VMEM((z.subs, lead, loads), BF16)])
        + [
            pltpu.VMEM(source.shape, F32),
            pltpu.VMEM(vectors_t.shape, BF16),
            pltpu.VMEM(panel.shape, BF16),
            pick,
            sems((8,)),
        ],
    )
    if z.folded:
        opening = exchange(*opening)
    else:
        opening = [lax.all_to_all(opening[0], "sub", 0, 0, tiled=True)]
    stack, first, second = run(
        part(static_kernel),
        [low(z.stack, order)]
        + [low(2 * side + modes, loads)] * 2,
        [operator_near, inverse_near, spot, vectors_t],
        scalars,
        [pick, sems(())],
    )
    left_static, right_static = exchange(first, second)
    sent = [shape(order, loads), Far(low(devices, modes, loads))]
    sent += [low(2 * side, loads)] * 2 + [low(side, loads)] * (1 if z.folded else 2)
    copies = pltpu.VMEM((devices, modes, loads), BF16)
    resid, every, first, second, *far = run(
        part(second_kernel),
        sent[:4] + [low(side + modes + z.wide, loads)] if z.folded else sent,
        [source, stack, *opening] + ([lent, panel] if z.folded else []),
        scalars,
        [copies, sems(())],
    )
    full = shape(order, loads)
    floor = pltpu.VMEM((order, loads), F32)
    solution = None
    for turn in range(ITERS):
        last = turn == ITERS - 1
        every = lax.all_to_all(every, ("sub", "grp"), 0, 0, tiled=True)
        left_got = lax.ppermute(first, "sub", ring(1))
        right_got = lax.ppermute(second, "sub", ring(-1))
        if z.folded:
            far_left = far_right = lax.ppermute(far[0], "sub", ring(2))
        else:
            far_left = lax.ppermute(far[0], "sub", ring(2))
            far_right = lax.ppermute(far[1], "sub", ring(-2))
        every = every.reshape(devices * modes, loads)
        args = [resid, inverse, operator]
        if turn:
            args += [error, coarse, stack]
            args += [solution] if turn > 1 else []
            outs = [full, full, Far(shape(owned, loads))]
            work = [square, square, floor, pltpu.VMEM((owned, loads), F32), sems((4,))]
        else:
            args += [*opening, lent, stack, spot, left_static, right_static]
            far_static = [far_left] if z.folded else []
            outs = [full, full, low(z.segments * side, 2 * z.window), low(order, 2 * side)]
            packed = low(z.window, z.subs * z.chunks * loads)
            outs += [] if z.folded else [packed]
            work = [square, square, pick, sems((3,))]
        error, product, *more = run(
            part(window_kernel, turn),
            outs,
            args,
            scalars,
            work,
            aliases={len(scalars) + 3: 0} if turn else None,
        )
        if turn:
            solution = Far(more[0])
        else:
            spread, columns, *panels = more
            panels = panels or [*opening, panel]
        args = [spot, every, *panels, spread, columns, product, resid]
        args += [first, second, left_got, right_got, far_left, far_right]
        args += [left_static, right_static, *far_static]
        if last:
            solution, resid = run(
                part(main_kernel, turn),
                [Far(shape(owned, loads))] * 2,
                args + [error, stack, solution],
                scalars,
                [pick, floor] + [pltpu.VMEM((owned, loads), F32)] * 3 + [sems((4,))],
            )
        else:
            gather = z.folded and not turn
            outs = sent + [packed] * gather + [low(z.window, loads), full]
            resid, every, first, second, *far, coarse, error = run(
                part(main_kernel, turn),
                outs,
                args + [error, stack],
                scalars,
                [pick, floor, copies, sems((3,))],
                aliases={len(scalars) + len(args): len(outs) - 1},
            )
            if gather:
                *far, panels = far
                panels = [panels]
    return (solution[None, None], resid[None, None])


def solution(mesh):
    return jax.shard_map(
        body,
        mesh=mesh,
        in_specs=(
            P("grp", "sub", None, None),
            P("grp", "sub"),
            P("grp", "sub", None),
            P("grp", "sub", None, None),
            P("grp", "sub", None, None),
            P("grp", "sub", None, None),
            P("grp", "sub"),
        ),
        out_specs=(P("grp", "sub", None, None), P("grp", "sub", None, None)),
        check_vma=False,
    )
```
